32 devices in a mesh: dp: 8 (over z, core), tensor: 4 (over y, x).
Axes of the slice: x: 2, y: 2, z: 4, core: 2. Of those that a mesh axis runs over, the one named last changes fastest.
Arguments:
- byte_in: bfloat16 [32, 4096, 768], P('dp', 'tensor'), may hold values from -6 to 6
- lengths: int32 [32], P('dp'), may hold values from 1024 to 4096, as said below
- latent: bfloat16 [256, 1280], P('tensor', 'dp'), may hold values from -6 to 6
- g_in: float32 [768], replicated, may hold values from 0.1 to 1.9
- b_in: float32 [768], replicated, may hold values from -3 to 3
- g_lat: float32 [1280], replicated, may hold values from 0.1 to 1.9
- b_lat: float32 [1280], replicated, may hold values from -3 to 3
- w_query: bfloat16 [1280, 256], P('dp', 'tensor'), may hold values from -0.15625 to 0.15625
- w_key: bfloat16 [768, 256], P('dp', 'tensor'), may hold values from -0.21875 to 0.21875
- w_value: bfloat16 [768, 1280], P('dp', 'tensor'), may hold values from -0.21875 to 0.21875
- w_out: bfloat16 [1280, 1280], P('tensor', 'dp'), may hold values from -6 to 6
- g_mlp: float32 [1280], replicated, may hold values from 0.1 to 1.9
- b_mlp: float32 [1280], replicated, may hold values from -3 to 3
- w_hidden: bfloat16 [1280, 1280], P('dp', 'tensor'), may hold values from -0.15625 to 0.15625
- b_hidden: float32 [1280], replicated, may hold values from -3 to 3
- w_back: bfloat16 [1280, 1280], P('tensor', 'dp'), may hold values from -0.15625 to 0.15625
- b_back: float32 [1280], replicated, may hold values from -3 to 3
- cotangent: float32 [32, 256, 1280], P('dp', 'tensor'), may hold values from -6 to 6
Outputs:
- latents_out: float32 [32, 256, 1280], P('dp', 'tensor')
- grad_bytes: float32 [32, 4096, 768], P('dp', 'tensor')
- grad_latent: float32 [256, 1280], P('tensor', 'dp')
- grad_g_in: float32 [768], replicated
- grad_b_in: float32 [768], replicated
- grad_g_lat: float32 [1280], replicated
- grad_b_lat: float32 [1280], replicated
- grad_w_query: float32 [1280, 256], P('dp', 'tensor')
- grad_w_key: float32 [768, 256], P('dp', 'tensor')
- grad_w_value: float32 [768, 1280], P('dp', 'tensor')
- grad_w_out: float32 [1280, 1280], P('tensor', 'dp')
- grad_g_mlp: float32 [1280], replicated
- grad_b_mlp: float32 [1280], replicated
- grad_w_hidden: float32 [1280, 1280], P('dp', 'tensor')
- grad_b_hidden: float32 [1280], replicated
- grad_w_back: float32 [1280, 1280], P('tensor', 'dp')
- grad_b_back: float32 [1280], replicated
The draws below stay inside these ranges and needn't reach their ends.
Inputs may be any that keep to these rules, and one draw needn't show every extreme that they name: Sequence b has live bytes at slots below lengths[b] and padding from there on; the first sequence is full.
All inputs are finite; a program needn't handle non-finite values.
Results may differ from the reference program's by a relative error of at most 0.019.
Values may be sent and summed in bfloat16 or wider, within the bound.
No kernel may reach another device: no remote copies, remote signals or barrier semaphores. Data moves between devices by JAX's collectives and lax.ppermute only.
A program may use at most 256 MiB of HBM per device.

```python
import jax
import jax.numpy as jnp
from jax import lax

C = 768
D = 1280
N = 256
H = 8
QK = 256
VC = 1280
FF = 1280
HQ = 32
HV = 160
LMAX = 4096
SEQS = 32


def draw_lengths(key, part):
    spans = jax.random.randint(key, (SEQS,), LMAX // 4, LMAX + 1, dtype=jnp.int32)
    return spans.at[0].set(LMAX)


def strengthened(entries, key, source, target, shards_of, factor):
    def block_of(position):
        return (jnp.arange(entries.shape[position]) // (entries.shape[position] // shards_of)).reshape((-1,) + (1,) * (entries.ndim - 1 - position))

    near = jax.random.permutation(key, shards_of)[block_of(target)]
    other_side = (block_of(target) + shards_of // 2) % shards_of
    return jnp.where((block_of(source) == near) | (block_of(source) == other_side), factor * entries, entries)


def levels(stream_key, extent, pieces, least, high):
    loudness, own = 1.0, jax.random.fold_in(stream_key, 6)
    for position, shards_of in pieces:
        draws = jnp.exp(jax.random.uniform(jax.random.fold_in(own, position), (shards_of,), jnp.float32, least / len(pieces), high / len(pieces)))
        loudness = loudness * jnp.repeat(draws, extent[position] // shards_of).reshape([-1 if axis == position else 1 for axis in range(len(extent))])
    return loudness


def bell_draw(stream_key, extent, width, most, split=(), held_as=jnp.bfloat16):
    drawn = width * jax.random.normal(stream_key, extent, jnp.float32)
    if split:
        drawn = drawn * levels(stream_key, extent, split, -0.22, 0.18)
    return jnp.clip(drawn, -most, most).astype(held_as)


def gaussian_with(own_key, extent, scale, limit, split, heavy, held_as=jnp.bfloat16):
    array = scale * jax.random.normal(own_key, extent, jnp.float32)
    if split:
        array = array * levels(own_key, extent, split, -0.22, 0.18)
    return jnp.clip(strengthened(array, jax.random.fold_in(own_key, 3), *heavy), -limit, limit).astype(held_as)


def setup_inputs(seed: int = 0) -> dict:
    key_of = jax.random.split(jax.random.key(seed), 19)
    byte_in = gaussian_with(key_of[0], (SEQS, LMAX, C), 1.0, 6.0, ((0, 8), (1, 4)), (0, 2, 8, 2.0))
    lengths = draw_lengths(jax.random.fold_in(key_of[18], 71), 0)
    latent = bell_draw(key_of[2], (N, D), 1.0, 6.0, ((0, 4), (1, 8)))
    g_in = jnp.clip(1.0 + 0.18 * jax.random.normal(key_of[3], (C,), jnp.float32), 0.1, 1.9)
    b_in = bell_draw(key_of[4], (C,), 0.5, 3.0, (), jnp.float32)
    g_lat = jnp.clip(1.0 + 0.18 * jax.random.normal(key_of[5], (D,), jnp.float32), 0.1, 1.9)
    b_lat = bell_draw(key_of[6], (D,), 0.5, 3.0, (), jnp.float32)
    w_query = bell_draw(key_of[7], (D, QK), D ** -0.5, 0.15625, ((0, 8), (1, 4)))
    w_key = bell_draw(key_of[8], (C, QK), C ** -0.5, 0.21875, ((0, 8), (1, 4)))
    w_value = bell_draw(key_of[9], (C, VC), C ** -0.5, 0.21875, ((0, 8), (1, 4)))
    w_out = bell_draw(key_of[10], (VC, D), (max(1, VC * 4 // LMAX)) ** -0.5, 6.0, ((0, 4), (1, 8)))
    g_mlp = jnp.clip(1.0 + 0.18 * jax.random.normal(key_of[11], (D,), jnp.float32), 0.1, 1.9)
    b_mlp = bell_draw(key_of[12], (D,), 0.5, 3.0, (), jnp.float32)
    w_hidden = bell_draw(key_of[13], (D, FF), D ** -0.5, 0.15625, ((0, 8), (1, 4)))
    b_hidden = bell_draw(key_of[14], (FF,), 0.5, 3.0, (), jnp.float32)
    w_back = bell_draw(key_of[15], (FF, D), FF ** -0.5, 0.15625, ((0, 4), (1, 8)))
    b_back = bell_draw(key_of[16], (D,), 0.5, 3.0, (), jnp.float32)
    cotangent = gaussian_with(key_of[17], (SEQS, N, D), 1.0, 6.0, ((0, 8), (1, 4)), (0, 2, 8, 2.0), jnp.float32)
    return dict(byte_in=byte_in, lengths=lengths, latent=latent, g_in=g_in, b_in=b_in, g_lat=g_lat, b_lat=b_lat, w_query=w_query, w_key=w_key, w_value=w_value, w_out=w_out, g_mlp=g_mlp, b_mlp=b_mlp, w_hidden=w_hidden, b_hidden=b_hidden, w_back=w_back, b_back=b_back, cotangent=cotangent)


@jax.custom_vjp
def low(v):
    return lax.optimization_barrier(v.astype(jnp.bfloat16)).astype(jnp.float32)

@jax.custom_vjp
def low_back(v):
    return v

def low_keep(v):
    return (low(v), None)

def low_pass(kept, grad):
    return (grad,)

def back_keep(v):
    return (v, None)

def back_low(kept, grad):
    return (low(grad),)
low.defvjp(low_keep, low_pass)
low_back.defvjp(back_keep, back_low)
HIGHEST_MODE = lax.Precision.HIGHEST
NEGATIVE = -1e+30

def normalize(values, gain, shift):
    center = lax.optimization_barrier(jnp.mean(values, axis=-1, keepdims=True))
    centered = values - center
    spread = lax.optimization_barrier(jnp.mean(centered * centered, axis=-1, keepdims=True))
    return centered * lax.rsqrt(spread + 1e-05) * gain + shift

def product(left, right):
    return jnp.matmul(left, right, precision=HIGHEST_MODE)

def attend(item):
    query_seq, keys_seq, values_seq, length = item
    query_heads = query_seq.reshape(N, H, HQ)
    key_heads = keys_seq.reshape(LMAX, H, HQ)
    value_heads = values_seq.reshape(LMAX, H, HV)
    raw = low_back(jnp.einsum('nhd,lhd->hnl', query_heads, key_heads, precision=HIGHEST_MODE))
    live = jnp.arange(LMAX, dtype=jnp.int32) < length
    scores = jnp.where(live[None, None, :], raw * HQ ** (-0.5), NEGATIVE)
    summit = lax.optimization_barrier(jnp.max(scores, axis=-1, keepdims=True))
    weights = jnp.exp(scores - summit)
    probs = weights / lax.optimization_barrier(jnp.sum(weights, axis=-1, keepdims=True))
    mixed = jnp.einsum('hnl,lhe->nhe', low(probs), value_heads, precision=HIGHEST_MODE)
    return low_back(low(mixed.reshape(N, VC)))

def forward(latent, g_in, b_in, g_lat, b_lat, w_query, w_key, w_value, w_out, g_mlp, b_mlp, w_hidden, b_hidden, w_back, b_back, byte_in, lengths):
    count = byte_in.shape[0]
    latent_wide = jnp.broadcast_to(latent, (count, N, D))
    latent_r = low(normalize(latent_wide, g_lat, b_lat))
    query = low_back(low(product(latent_r, w_query)))
    bytes_r = low(normalize(byte_in, g_in, b_in))
    keys = low_back(low(product(bytes_r, w_key)))
    values = low_back(low(product(bytes_r, w_value)))
    mixed = lax.map(jax.checkpoint(attend), (query, keys, values, lengths))
    latent_mid = latent_wide + low_back(product(mixed, w_out))
    hidden_r = low(normalize(latent_mid, g_mlp, b_mlp))
    pre = low_back(product(hidden_r, w_hidden) + b_hidden)
    act_r = low(jax.nn.gelu(pre, approximate=False))
    return latent_mid + low_back(product(act_r, w_back)) + b_back

def reference(byte_in, lengths, latent, g_in, b_in, g_lat, b_lat, w_query, w_key, w_value, w_out, g_mlp, b_mlp, w_hidden, b_hidden, w_back, b_back, cotangent):
    params = (latent.astype(jnp.float32), g_in, b_in, g_lat, b_lat, w_query.astype(jnp.float32), w_key.astype(jnp.float32), w_value.astype(jnp.float32), w_out.astype(jnp.float32), g_mlp, b_mlp, w_hidden.astype(jnp.float32), b_hidden, w_back.astype(jnp.float32), b_back, byte_in.astype(jnp.float32))

    def runner(*inputs):
        return forward(*inputs, lengths)
    result, pullback = jax.vjp(runner, *params)
    grads = pullback(cotangent)
    grad_latent, grad_g_in, grad_b_in, grad_g_lat, grad_b_lat, grad_w_query, grad_w_key, grad_w_value, grad_w_out, grad_g_mlp, grad_b_mlp, grad_w_hidden, grad_b_hidden, grad_w_back, grad_b_back, grad_bytes = grads
    return (result, grad_bytes, grad_latent, grad_g_in, grad_b_in, grad_g_lat, grad_b_lat, grad_w_query, grad_w_key, grad_w_value, grad_w_out, grad_g_mlp, grad_b_mlp, grad_w_hidden, grad_b_hidden, grad_w_back, grad_b_back)
```

```python
from functools import partial
import math

import jax
import jax.numpy as jnp
from jax import lax
from jax.experimental import pallas as pl
from jax.experimental.pallas import tpu as pltpu
from jax.sharding import PartitionSpec as P

HQ = 32
HV = 160
EPS = 1e-05
NEGATIVE = -1e30
SCALE = HQ**-0.5
LOG2E = math.log2(math.e)
SCALE2 = SCALE * LOG2E
BF = jnp.bfloat16
F32 = jnp.float32
VMEM_LIMIT = 60 << 20


def up128(n):
    return (n + 127) // 128 * 128


def nn(a, b):
    return lax.dot_general(a, b, (((1,), (0,)), ((), ())), preferred_element_type=F32)


def nt(a, b):
    return lax.dot_general(a, b, (((1,), (1,)), ((), ())), preferred_element_type=F32)


def tn(a, b):
    return lax.dot_general(a, b, (((0,), (0,)), ((), ())), preferred_element_type=F32)


def cost(flops, nbytes, trans=0):
    return pl.CostEstimate(flops=int(flops), bytes_accessed=int(nbytes), transcendentals=int(trans))


def params(n_axes):
    sem = ("arbitrary",) * n_axes if n_axes else None
    return pltpu.CompilerParams(dimension_semantics=sem, vmem_limit_bytes=VMEM_LIMIT)


class Blocks:
    def __init__(self, heads):
        self.heads = heads
        self.width = up128(heads * (HV + HQ))
        self.vals = heads * HV
        self.k0 = self.vals // 128 * 128
        self.kw = self.width - self.k0

    def window(self, i):
        first = i * HV
        start = first // 128 * 128
        return first, start, up128(first + HV - start)


def lanes(shape, start=0):
    return lax.broadcasted_iota(jnp.int32, shape, len(shape) - 1) + start


def three_terms(x):
    hi = x.astype(BF).astype(F32)
    mid = (x - hi).astype(BF).astype(F32)
    lo = (x - hi - mid).astype(BF).astype(F32)
    return hi, mid, lo


def norm_kernel(x_ref, g_ref, b_ref, r_ref, xh_ref, s_ref):
    x = x_ref[0].astype(F32)
    mu = jnp.mean(x, axis=1, keepdims=True)
    xc = x - mu
    rstd = lax.rsqrt(jnp.mean(xc * xc, axis=1, keepdims=True) + EPS)
    xh = xc * rstd
    r_ref[0] = (xh * g_ref[...] + b_ref[...]).astype(BF)
    xh_ref[0] = xh.astype(BF)
    s_ref[0] = jnp.broadcast_to(rstd, s_ref.shape[1:])


def byte_norm(x, g, b):
    seqs, slots, width = x.shape
    tile = min(512, slots)
    row = lambda s, l: (s, l, 0)
    full = pl.BlockSpec((1, width), lambda s, l: (0, 0))
    return pl.pallas_call(
        norm_kernel,
        grid=(seqs, slots // tile),
        in_specs=[pl.BlockSpec((1, tile, width), row), full, full],
        out_specs=[
            pl.BlockSpec((1, tile, width), row),
            pl.BlockSpec((1, tile, width), row),
            pl.BlockSpec((1, tile, 128), row),
        ],
        out_shape=[
            jax.ShapeDtypeStruct(x.shape, BF),
            jax.ShapeDtypeStruct(x.shape, BF),
            jax.ShapeDtypeStruct((seqs, slots, 128), F32),
        ],
        compiler_params=params(2),
        cost_estimate=cost(10 * x.size, 6 * x.size),
        name="byte_norm",
    )(x, g.reshape(1, -1), b.reshape(1, -1))


def fwd_kernel(blk, parts, live_ref, b_ref, w_ref, q_ref, kv_ref, p_ref, y_ref, m_ref, acc, cs):
    s = pl.program_id(0)
    n = acc.shape[0]
    nl = n // parts
    slots = b_ref.shape[1]
    seqs = kv_ref.shape[0] * pl.num_programs(0)
    kv_ref[0] = nn(b_ref[0], w_ref[...]).astype(BF)
    mask = lanes((n, slots)) < live_ref[s]
    acc[...] = jnp.zeros_like(acc)
    stats = []
    for i in range(blk.heads):
        first, start, width = blk.window(i)
        rows = slice(i * n, (i + 1) * n)
        sc = nt(q_ref[rows], kv_ref[0, :, blk.k0 :])
        sc = jnp.where(mask, sc, NEGATIVE)
        top = jnp.max(sc, axis=1, keepdims=True)
        p = jnp.exp2((sc - top) * SCALE2)
        total = jnp.sum(p, axis=1, keepdims=True)
        p_ref[0, rows] = p.astype(BF)
        o = nn(p_ref[0, rows], kv_ref[0, :, start : start + width])
        at = lanes((n, width), start)
        acc[:, start : start + width] += jnp.where((at >= first) & (at < first + HV), o / total, 0.0)
        top = top * SCALE2
        m_ref[0, rows] = jnp.broadcast_to(top, (n, 128))
        stats.append(top + jnp.log(total) * LOG2E)
    y = acc[...]
    center = jnp.mean(y, axis=0, keepdims=True).astype(BF).astype(F32)
    y = y - center
    at = lanes(y.shape)
    for i, lse in enumerate(stats):
        for j, term in enumerate(three_terms(lse)):
            y = jnp.where(at == blk.vals + 3 * i + j, term, y)
    y = y.astype(BF)
    for k in range(parts):
        y_ref[k, pl.ds(pl.multiple_of(s * nl, nl), nl), :] = y[k * nl : (k + 1) * nl]
    cs[...] = jnp.where(lax.broadcasted_iota(jnp.int32, cs.shape, 0) == s, center, cs[...])

    @pl.when(s == pl.num_programs(0) - 1)
    def _():
        rows = lax.broadcasted_iota(jnp.int32, cs.shape, 0)
        c = jnp.where(rows < pl.num_programs(0), cs[...], 0.0).astype(BF)
        for k in range(parts):
            y_ref[k, y_ref.shape[1] - 16 :, :] = c


def attend(blk, parts, live, bytes_r, w, q):
    seqs, slots, width = bytes_r.shape
    n = q.shape[0] // blk.heads
    rows = seqs * (n // parts) + 16
    seq = lambda s, live: (s, 0, 0)
    flops = 2 * seqs * slots * (width * blk.width + blk.heads * n * (blk.kw + 256))
    return pl.pallas_call(
        partial(fwd_kernel, blk, parts),
        grid_spec=pltpu.PrefetchScalarGridSpec(
            num_scalar_prefetch=1,
            grid=(seqs,),
            in_specs=[
                pl.BlockSpec((1, slots, width), seq),
                pl.BlockSpec(w.shape, lambda s, live: (0, 0)),
                pl.BlockSpec(q.shape, lambda s, live: (0, 0)),
            ],
            out_specs=[
                pl.BlockSpec((1, slots, blk.width), seq),
                pl.BlockSpec((1, blk.heads * n, slots), seq),
                pl.BlockSpec((parts, rows, blk.width), lambda s, live: (0, 0, 0)),
                pl.BlockSpec((1, blk.heads * n, 128), seq),
            ],
            scratch_shapes=[pltpu.VMEM((n, blk.width), F32), pltpu.VMEM((16, blk.width), F32)],
        ),
        out_shape=[
            jax.ShapeDtypeStruct((seqs, slots, blk.width), BF),
            jax.ShapeDtypeStruct((seqs, blk.heads * n, slots), BF),
            jax.ShapeDtypeStruct((parts, rows, blk.width), BF),
            jax.ShapeDtypeStruct((seqs, blk.heads * n, 128), F32),
        ],
        compiler_params=params(1),
        cost_estimate=cost(flops, 4 * seqs * slots * width, seqs * blk.heads * n * slots),
        name="attend_forward",
    )(live, bytes_r, w, q)


def rows_kernel(blk, parts, seqs, *refs):
    me_ref, *refs = refs
    pays = [[refs[k * parts + j] for j in range(parts)] for k in range(parts)]
    refs = refs[parts * parts :]
    lat_ref, cot_ref, g_ref, b_ref, bh_ref, bb_ref, w_hbm = refs[:7]
    out_ref, pay_ref, lx_ref, rx_ref, vec_ref, dbh_ref, dsum_ref = refs[7:14]
    w_ref, mix, st, mid_s, acc, sems = refs[14:]
    me = me_ref[0]
    rows, d = acc.shape
    nl = rows // seqs
    piece = w_hbm.shape[1] // 3
    dps = w_hbm.shape[0] // parts

    def copies(m):
        for t in range(parts):
            for z in range(dps):
                yield pltpu.make_async_copy(
                    w_hbm.at[t * dps + z, pl.ds(m * piece, piece)],
                    w_ref.at[m, t, pl.ds(z * piece, piece)],
                    sems.at[m],
                )

    for m in (1, 0, 2):
        for c in copies(m):
            c.start()
    for j in range(parts):
        lses = []
        for k in range(parts):
            ref = pays[k ^ j][k]
            tail = ref[: seqs * nl, blk.k0 :].astype(F32)
            at = lanes(tail.shape, blk.k0)
            lses.append(
                [
                    jnp.sum(
                        jnp.where((at >= blk.vals + 3 * i) & (at < blk.vals + 3 * i + 3), tail, 0.0),
                        axis=1,
                        keepdims=True,
                    )
                    for i in range(blk.heads)
                ]
            )
        stat = jnp.zeros((rows, blk.kw), F32)
        at = lanes(stat.shape, blk.k0)
        weights = []
        for i in range(blk.heads):
            top = lses[0][i]
            for k in range(1, parts):
                top = jnp.maximum(top, lses[k][i])
            es = [jnp.exp2(lses[k][i] - top) for k in range(parts)]
            total = sum(es[1:], es[0])
            weights.append([e / total for e in es])
            lse = top + jnp.log(total) * LOG2E
            for q, term in enumerate(three_terms(lse)):
                stat = jnp.where(at == blk.vals + 6 * i + q, term, stat)
        st[j] = stat
        for s in range(seqs):
            sl = slice(s * nl, (s + 1) * nl)
            at = lanes((nl, blk.width))
            m = jnp.zeros((nl, blk.width), F32)
            for k in range(parts):
                ref = pays[k ^ j][k]
                y = ref[sl, :].astype(F32) + ref[seqs * nl + s : seqs * nl + s + 1, :].astype(F32)
                wt = jnp.zeros((nl, blk.width), F32)
                for i in range(blk.heads):
                    wt = jnp.where((at >= i * HV) & (at < (i + 1) * HV), weights[i][k][sl], wt)
                m = m + jnp.where(at < blk.vals, y * wt, 0.0)
            mix[j, sl] = m
            rx_ref[1, j, sl] = m.astype(BF)

    for m in (1, 0, 2):
        for c in copies(m):
            c.wait()

    acc[...] = jnp.zeros_like(acc)

    @pl.loop(0, parts)
    def _(j):
        acc[...] += nt(rx_ref[1, j], w_ref[1, me ^ j])

    for s in range(seqs):
        sl = slice(s * nl, (s + 1) * nl)
        mid_s[sl] = acc[sl] + lat_ref[...].astype(F32)
    mid = mid_s[...]
    mu = jnp.mean(mid, axis=1, keepdims=True)
    xc = mid - mu
    rstd = lax.rsqrt(jnp.mean(xc * xc, axis=1, keepdims=True) + EPS)
    lx_ref[0] = (xc * rstd * g_ref[...] + b_ref[...]).astype(BF)
    lx_ref[2] = cot_ref[...].astype(BF)
    acc[...] = jnp.zeros_like(acc)
    out_ref[...] = mid_s[...] + bb_ref[...]

    @pl.loop(0, parts)
    def _(j):
        t = me ^ j
        pre = nn(lx_ref[0], w_ref[0, t]) + bh_ref[t]
        phi = 0.5 * (1.0 + lax.erf(pre * math.sqrt(0.5)))
        slope = phi + pre * (jnp.exp(-0.5 * pre * pre) * (1.0 / math.sqrt(2.0 * math.pi)))
        rx_ref[2, j] = (pre * phi).astype(BF)
        dpre = (nn(lx_ref[2], w_ref[2, t]) * slope).astype(BF)
        rx_ref[0, j] = dpre
        dbh_ref[t] = jnp.sum(dpre.astype(F32), axis=0, keepdims=True)
        out_ref[...] += nt(rx_ref[2, j], w_ref[2, t])
        acc[...] += nt(rx_ref[0, j], w_ref[0, t])

    mid = mid_s[...]
    mu = jnp.mean(mid, axis=1, keepdims=True)
    xc = mid - mu
    rstd = lax.rsqrt(jnp.mean(xc * xc, axis=1, keepdims=True) + EPS)
    xh = xc * rstd
    dy = acc[...]
    vec_ref[0:1] = jnp.sum(dy * xh, axis=0, keepdims=True)
    vec_ref[1:2] = jnp.sum(dy, axis=0, keepdims=True)
    vec_ref[2:3] = jnp.sum(cot_ref[...], axis=0, keepdims=True)
    e = dy * g_ref[...]
    dv = rstd * (
        e - jnp.mean(e, axis=1, keepdims=True) - xh * jnp.mean(e * xh, axis=1, keepdims=True)
    )
    acc[...] = cot_ref[...] + dv
    lx_ref[1] = acc[...].astype(BF)
    total = acc[0:nl]
    for s in range(1, seqs):
        total = total + acc[s * nl : (s + 1) * nl]
    dsum_ref[...] = total

    @pl.loop(0, parts)
    def _(j):
        dm = nn(lx_ref[1], w_ref[1, me ^ j]).astype(BF)
        prod = dm.astype(F32) * mix[j]
        at = lanes(prod.shape)
        stat = st[j]
        at_k = lanes(stat.shape, blk.k0)
        for i in range(blk.heads):
            inner = jnp.sum(
                jnp.where((at >= i * HV) & (at < (i + 1) * HV), prod, 0.0), axis=1, keepdims=True
            )
            for q, term in enumerate(three_terms(inner)):
                stat = jnp.where(at_k == blk.vals + 6 * i + 3 + q, term, stat)
        if blk.k0:
            pay_ref[j, :, : blk.k0] = dm[:, : blk.k0]
        pay_ref[j, :, blk.k0 :] = jnp.where(at_k < blk.vals, dm[:, blk.k0 :].astype(F32), stat).astype(BF)


def rows_step(blk, parts, seqs, me, pays, lat, cot, g, b, bh, bb, w):
    rows, d = cot.shape
    flat = [a for stage in pays for a in stage]
    nl = rows // seqs
    vm = pl.BlockSpec(memory_space=pltpu.VMEM)
    own = pl.BlockSpec((None,) + flat[0].shape[1:], lambda i, me: (0, 0, 0))
    whole = lambda a: pl.BlockSpec(a.shape, lambda i, me, r=a.ndim: (0,) * r)
    outs = [
        jax.ShapeDtypeStruct((rows, d), F32),
        jax.ShapeDtypeStruct((parts, rows, blk.width), BF),
        jax.ShapeDtypeStruct((3, rows, d), BF),
        jax.ShapeDtypeStruct((3, parts, rows, blk.width), BF),
        jax.ShapeDtypeStruct((8, d), F32),
        jax.ShapeDtypeStruct((parts, 1, blk.width), F32),
        jax.ShapeDtypeStruct((nl, d), F32),
    ]
    return pl.pallas_call(
        partial(rows_kernel, blk, parts, seqs),
        grid_spec=pltpu.PrefetchScalarGridSpec(
            num_scalar_prefetch=1,
            grid=(1,),
            in_specs=[own if a.ndim == 3 else whole(a) for a in flat]
            + [whole(a) for a in (lat, cot, g, b, bh, bb)]
            + [pl.BlockSpec(memory_space=pl.ANY)],
            out_specs=[whole(o) for o in outs],
            scratch_shapes=[
                pltpu.VMEM((3, parts, d, blk.width), BF),
                pltpu.VMEM((parts, rows, blk.width), F32),
                pltpu.VMEM((parts, rows, blk.kw), F32),
                pltpu.VMEM((rows, d), F32),
                pltpu.VMEM((rows, d), F32),
                pltpu.SemaphoreType.DMA((3,)),
            ],
        ),
        out_shape=outs,
        compiler_params=params(1),
        cost_estimate=cost(12 * rows * d * d, 2 * w.size + 40 * rows * d, 2 * rows * d),
        name="rows",
    )(me, *flat, lat, cot, g, b, bh, bb, w)


def weights_kernel(core_ref, lx_ref, rx_ref, lx2_ref, rx2_ref, out_ref):
    r = tn(lx_ref[0], rx_ref[0, 0]) + tn(lx2_ref[0], rx2_ref[0, 0])
    out_ref[0, :, 0] = r.astype(BF).reshape(out_ref.shape[1], out_ref.shape[3], out_ref.shape[4])


def weight_grads(core, dps, lx, rx, lx2, rx2):
    _, parts, rows, width = rx.shape
    d = lx.shape[2]
    half = max(parts // 2, 1)
    lspec = pl.BlockSpec((1, rows, d), lambda m, i, c: (m, 0, 0))
    rspec = pl.BlockSpec((1, 1, rows, width), lambda m, i, c: (m, c[0] * half + i, 0, 0))
    return pl.pallas_call(
        weights_kernel,
        grid_spec=pltpu.PrefetchScalarGridSpec(
            num_scalar_prefetch=1,
            grid=(3, half),
            in_specs=[lspec, rspec, lspec, rspec],
            out_specs=pl.BlockSpec((1, dps, 1, d // dps, width), lambda m, i, c: (i, 0, m, 0, 0)),
        ),
        out_shape=jax.ShapeDtypeStruct((half, dps, 3, d // dps, width), BF),
        compiler_params=params(2),
        cost_estimate=cost(12 * half * rows * d * width, 6 * half * d * width),
        name="weight_grads",
    )(core, lx, rx, lx2, rx2)


def bwd_kernel(blk, parts, *refs):
    kv_ref, p_ref, m_ref, xh_ref, q_ref, w_ref, g_ref, b_ref, *refs = refs
    dms = refs[:parts]
    dkv_ref, gw_ref, dq_ref, dgb_ref, dkvt, gacc, sacc, dmx = refs[parts:]
    s = pl.program_id(0)
    n = dmx.shape[0]
    nl = n // parts

    @pl.when(s == 0)
    def _():
        gacc[...] = jnp.zeros_like(gacc)
        sacc[...] = jnp.zeros_like(sacc)
        dq_ref[...] = jnp.zeros_like(dq_ref)

    for k in range(parts):
        dmx[k * nl : (k + 1) * nl] = dms[k][...].reshape(nl, blk.width)
    tail = dmx[:, blk.k0 :].astype(F32)
    at_k = lanes(tail.shape, blk.k0)

    def stat(i, q):
        lo = blk.vals + 6 * i + 3 * q
        return jnp.sum(jnp.where((at_k >= lo) & (at_k < lo + 3), tail, 0.0), axis=1, keepdims=True)

    dkvt[...] = jnp.zeros_like(dkvt)
    for i in range(blk.heads):
        first, start, width = blk.window(i)
        rows = slice(i * n, (i + 1) * n)
        ratio = jnp.exp2(m_ref[0, rows, 0:1] - stat(i, 0))
        inner = stat(i, 1)
        at = lanes((n, width), start)
        dm = dmx[:, start : start + width].astype(F32)
        dm = jnp.where((at >= first) & (at < first + HV), dm, 0.0)
        dp = nt(dm.astype(BF), kv_ref[0, :, start : start + width])
        ds = (p_ref[0, rows].astype(F32) * ((dp - inner) * (ratio * SCALE))).astype(BF)
        dkvt[start : start + width, :] += tn((dm * ratio).astype(BF), p_ref[0, rows])
        dkvt[blk.k0 :, :] += tn(q_ref[rows], ds)
        dq = nn(ds, kv_ref[0, :, blk.k0 :])
        key = blk.vals + i * HQ
        dq_ref[...] += jnp.where((at_k >= key) & (at_k < key + HQ), dq, 0.0)
    low = dkvt[...].astype(BF)
    dkv_ref[0] = low.T
    gacc[...] += nn(low, xh_ref[0])
    sacc[...] += jnp.sum(low.astype(F32), axis=1, keepdims=True)

    @pl.when(s == pl.num_programs(0) - 1)
    def _():
        wt = w_ref[...].T.astype(F32)
        grad, col = gacc[...], sacc[:, 0:1]
        dgb_ref[0:1] = jnp.sum(wt * grad, axis=0, keepdims=True)
        dgb_ref[1:2] = jnp.sum(wt * col, axis=0, keepdims=True)
        gw_ref[...] = (grad * g_ref[...] + col * b_ref[...]).T.astype(BF)


def attend_backward(blk, parts, stage, kv, p, m, xh, q, w, g, b, pays):
    seqs, slots, width = xh.shape
    n = q.shape[0] // blk.heads
    nl = n // parts
    seq = lambda s: (s, 0, 0)
    flat = lambda s: (0, 0)
    specs = [
        pl.BlockSpec((None, nl, blk.width), lambda s: (stage, s, 0))
        if a.ndim == 3
        else pl.BlockSpec((nl, blk.width), lambda s: (s, 0))
        for a in pays
    ]
    return pl.pallas_call(
        partial(bwd_kernel, blk, parts),
        grid=(seqs,),
        in_specs=[
            pl.BlockSpec((1, slots, blk.width), seq),
            pl.BlockSpec((1, blk.heads * n, slots), seq),
            pl.BlockSpec((1, blk.heads * n, 128), seq),
            pl.BlockSpec((1, slots, width), seq),
            pl.BlockSpec(q.shape, flat),
            pl.BlockSpec(w.shape, flat),
            pl.BlockSpec((1, width), flat),
            pl.BlockSpec((1, width), flat),
            *specs,
        ],
        out_specs=[
            pl.BlockSpec((1, slots, blk.width), seq),
            pl.BlockSpec((width, blk.width), flat),
            pl.BlockSpec((n, blk.kw), flat),
            pl.BlockSpec((8, width), flat),
        ],
        out_shape=[
            jax.ShapeDtypeStruct((seqs, slots, blk.width), BF),
            jax.ShapeDtypeStruct((width, blk.width), BF),
            jax.ShapeDtypeStruct((n, blk.kw), F32),
            jax.ShapeDtypeStruct((8, width), F32),
        ],
        scratch_shapes=[
            pltpu.VMEM((blk.width, slots), F32),
            pltpu.VMEM((blk.width, width), F32),
            pltpu.VMEM((blk.width, 128), F32),
            pltpu.VMEM((n, blk.width), BF),
        ],
        compiler_params=params(1),
        cost_estimate=cost(
            2 * seqs * slots * (width * blk.width + 4 * blk.heads * n * 256), 6 * seqs * slots * width
        ),
        name="attend_backward",
    )(kv, p, m, xh, q, w, g, b, *pays)


def bytes_kernel(parts, *refs):
    dkvs, ws = refs[:parts], refs[parts : 2 * parts]
    xh_ref, s_ref, g_ref, out_ref = refs[2 * parts :]
    dy = nt(dkvs[0][0], ws[0][...])
    for k in range(1, parts):
        dy = dy + nt(dkvs[k][0], ws[k][...])
    xh = xh_ref[0].astype(F32)
    e = dy * g_ref[...]
    me = jnp.mean(e, axis=1, keepdims=True)
    mx = jnp.mean(e * xh, axis=1, keepdims=True)
    out_ref[0] = s_ref[0, :, 0:1] * (e - me - xh * mx)


def byte_grads(dkvs, ws, xh, rstd, g):
    seqs, slots, width = xh.shape
    bw = ws[0].shape[1]
    tile = min(512, slots)
    row = lambda s, l: (s, l, 0)
    flat = lambda s, l: (0, 0)
    return pl.pallas_call(
        partial(bytes_kernel, len(ws)),
        grid=(seqs, slots // tile),
        in_specs=[pl.BlockSpec((1, tile, bw), row) for _ in dkvs]
        + [pl.BlockSpec((width, bw), flat) for _ in ws]
        + [
            pl.BlockSpec((1, tile, width), row),
            pl.BlockSpec((1, tile, 128), row),
            pl.BlockSpec((1, width), flat),
        ],
        out_specs=pl.BlockSpec((1, tile, width), row),
        out_shape=jax.ShapeDtypeStruct(xh.shape, F32),
        compiler_params=params(2),
        cost_estimate=cost(2 * xh.size * bw * len(ws), 10 * xh.size),
        name="byte_grads",
    )(*dkvs, *ws, xh, rstd, g)


def on_device(
    dps,
    parts,
    byte_in,
    lengths,
    latent,
    g_in,
    b_in,
    g_lat,
    b_lat,
    w_query,
    w_key,
    w_value,
    w_out,
    g_mlp,
    b_mlp,
    w_hidden,
    b_hidden,
    w_back,
    b_back,
    cotangent,
):
    seqs, slots, width = byte_in.shape
    nl, dl = latent.shape
    n, d = nl * parts, dl * dps
    blk = Blocks(w_key.shape[1] // HQ)
    qk = w_key.shape[1]
    bw = blk.width
    me = lax.axis_index("tensor").astype(jnp.int32)
    dp = lax.axis_index("dp").astype(jnp.int32)
    core = dp % 2

    def hop(x, k):
        return lax.ppermute(x, "tensor", [(i, i ^ k) for i in range(parts)])

    def hop_dp(x, k):
        return lax.ppermute(x, "dp", [(i, i ^ k) for i in range(dps)])

    def widen(x):
        return jnp.pad(x, ((0, 0), (0, bw - x.shape[1])))

    kv_shard = widen(jnp.concatenate([w_value, w_key], axis=1))
    lq_shard = jnp.concatenate([latent.T, w_query], axis=1)
    kv_own = lax.all_gather(kv_shard, "dp", axis=0, tiled=True)
    lq_own = lax.all_gather(lq_shard, "dp", axis=0, tiled=True)
    lqs = [lq_own] + [hop(lq_own, k) for k in range(1, parts)]
    ws = [kv_own] + [hop(kv_own, k) for k in range(1, parts)]
    mats = jnp.concatenate([widen(w_hidden), widen(w_out.T), widen(w_back.T)], axis=0)
    mats = lax.all_gather(mats, ("tensor", "dp"), axis=0, tiled=False)

    bytes_r, xh, rstd = byte_norm(byte_in, g_in, b_in)

    lat_t = jnp.concatenate([a[:, :nl] for a in lqs], axis=1).astype(F32)
    wq = jnp.concatenate([a[:, nl:] for a in lqs], axis=1)
    mu = jnp.mean(lat_t, axis=0, keepdims=True)
    lat_c = lat_t - mu
    lat_s = lax.rsqrt(jnp.mean(lat_c * lat_c, axis=0, keepdims=True) + EPS)
    lat_h = lat_c * lat_s
    lat_r = (lat_h * g_lat[:, None] + b_lat[:, None]).astype(BF)
    query = tn(lat_r, wq).astype(BF)
    qs = []
    for k in range(parts):
        part = jnp.pad(query[:, k * qk : (k + 1) * qk], ((0, 0), (blk.vals - blk.k0, bw - blk.vals - qk)))
        at = lanes(part.shape, blk.k0)
        qs.append(
            jnp.concatenate(
                [
                    jnp.where((at >= blk.vals + i * HQ) & (at < blk.vals + (i + 1) * HQ), part, 0)
                    for i in range(blk.heads)
                ],
                axis=0,
            )
        )

    live = jnp.clip(lengths - me * slots, 0, slots).astype(jnp.int32)
    kvs, ps, ms, pays = [], [], [], []
    for k in range(parts):
        kv, p, y, m = attend(blk, parts, live, bytes_r, ws[k], qs[k])
        kvs.append(kv)
        ps.append(p)
        ms.append(m)
        pays.append([y] + [hop(y[j], j) for j in range(1, parts)])

    rows = seqs * nl
    bh = jnp.pad(b_hidden.reshape(parts, 1, -1), ((0, 0), (0, 0), (0, bw - d // parts)))
    out, dpay, lx, rx, vecs, dbh, dsum = rows_step(
        blk,
        parts,
        seqs,
        me.reshape(1),
        pays,
        lq_own[:, :nl].T,
        cotangent.reshape(rows, d),
        g_mlp.reshape(1, -1),
        b_mlp.reshape(1, -1),
        bh,
        b_back.reshape(1, -1),
        mats,
    )
    latents_out = out.reshape(seqs, nl, d)
    order = list(range(1, parts)) + [0]
    dpays = {k: [dpay] + [hop(dpay[j ^ k], j) for j in range(1, parts)] for k in order}
    lx2, rx2 = hop_dp(lx, 1), hop_dp(rx, 1)
    grads = weight_grads(core.reshape(1), dps, lx, rx, lx2, rx2)
    half = grads.shape[0]
    total = None
    for i in range(half):
        perm = [
            (z * parts + t, z * parts + (t ^ ((z % 2) * half + i))) for z in range(dps) for t in range(parts)
        ]
        got = lax.ppermute(grads[i], ("dp", "tensor"), perm).astype(F32)
        total = got if total is None else total + got
    grad_mats = lax.psum_scatter(
        total.astype(BF).reshape(dps, -1, bw), "dp", scatter_dimension=0, tiled=True
    ).reshape(3, dl, bw)
    grad_mats = grad_mats[:, :, : d // parts].astype(F32)
    grad_sum = lax.psum_scatter(dsum.astype(BF), "dp", scatter_dimension=1, tiled=True).astype(F32)

    dkvs, dqs, gw, dgb = [None] * parts, [None] * parts, None, None
    for k in order:
        dkvs[k], grad, dq, dgb_k = attend_backward(
            blk, parts, k, kvs[k], ps[k], ms[k], xh, qs[k], ws[k], g_in[None], b_in[None], dpays[k]
        )
        dqs[k] = dq[:, blk.vals - blk.k0 : blk.vals - blk.k0 + qk]
        dgb = dgb_k if dgb is None else dgb + dgb_k
        grad = (hop(grad, k) if k else grad).astype(F32)
        gw = grad if gw is None else gw + grad
    grad_kv = lax.psum_scatter(gw.astype(BF), "dp", scatter_dimension=0, tiled=True).astype(F32)

    dq = jnp.concatenate(dqs, axis=1).reshape(parts, nl, parts, qk)
    vec = jnp.concatenate(
        [dgb[:2].reshape(-1), vecs[:3].reshape(-1), dbh[:, 0, : d // parts].reshape(-1)]
    )
    vec = jnp.pad(vec, (0, (-vec.size) % 1024)).reshape(-1, 128)
    j = 1
    while j < parts:
        other = [i ^ j for i in range(parts)]
        got = hop(dq, j)
        got = jnp.stack([got[i] for i in other], axis=0)
        got = jnp.stack([got[:, :, i] for i in other], axis=2)
        dq = dq + got
        vec = vec + hop(vec, j)
        j *= 2
    j = 1
    while j < dps:
        dq = dq + hop_dp(dq, j)
        vec = vec + hop_dp(vec, j)
        j *= 2
    vec = vec.reshape(-1)
    cuts = [width, width, d, d, d, d]
    pieces, at = [], 0
    for c in cuts:
        pieces.append(vec[at : at + c])
        at += c
    sum_g_in, sum_b_in, sum_g_mlp, sum_b_mlp, sum_back, sum_hidden = pieces

    grad_bytes = byte_grads(dkvs, ws, xh, rstd, g_in[None])

    dq = dq.reshape(n, parts * qk).astype(BF)
    mine = lax.dynamic_slice_in_dim(lat_r, dp * dl, dl, 0)
    grad_w_query = nn(mine, dq[:, :qk])
    dlat = nt(wq, dq)
    sum_g_lat = jnp.sum(dlat * lat_h, axis=1)
    sum_b_lat = jnp.sum(dlat, axis=1)
    e = dlat[:, :nl] * g_lat[:, None]
    eh = lat_h[:, :nl]
    dv = lat_s[:, :nl] * (
        e - jnp.mean(e, axis=0, keepdims=True) - eh * jnp.mean(e * eh, axis=0, keepdims=True)
    )
    grad_latent = grad_sum + lax.dynamic_slice_in_dim(dv, dp * dl, dl, 0).T

    return (
        latents_out,
        grad_bytes,
        grad_latent,
        sum_g_in,
        sum_b_in,
        sum_g_lat,
        sum_b_lat,
        grad_w_query,
        grad_kv[:, blk.vals : blk.vals + qk],
        grad_kv[:, : blk.vals],
        grad_mats[1].T,
        sum_g_mlp,
        sum_b_mlp,
        grad_mats[0],
        sum_hidden,
        grad_mats[2].T,
        sum_back,
    )


def solution(mesh):
    return jax.shard_map(
        partial(on_device, mesh.shape["dp"], mesh.shape["tensor"]),
        mesh=mesh,
        in_specs=(
            P("dp", "tensor", None),
            P("dp"),
            P("tensor", "dp"),
            P(),
            P(),
            P(),
            P(),
            P("dp", "tensor"),
            P("dp", "tensor"),
            P("dp", "tensor"),
            P("tensor", "dp"),
            P(),
            P(),
            P("dp", "tensor"),
            P(),
            P("tensor", "dp"),
            P(),
            P("dp", "tensor", None),
        ),
        out_specs=(
            P("dp", "tensor", None),
            P("dp", "tensor", None),
            P("tensor", "dp"),
            P(),
            P(),
            P(),
            P(),
            P("dp", "tensor"),
            P("dp", "tensor"),
            P("dp", "tensor"),
            P("tensor", "dp"),
            P(),
            P(),
            P("dp", "tensor"),
            P(),
            P("tensor", "dp"),
            P(),
        ),
        check_vma=False,
    )
```

```python
from functools import partial
import math

import jax
import jax.numpy as jnp
from jax import lax
from jax.experimental import pallas as pl
from jax.experimental.pallas import tpu as pltpu
from jax.sharding import PartitionSpec as P

HQ = 32
HV = 160
EPS = 1e-05
NEGATIVE = -1e30
SCALE = HQ**-0.5
LOG2E = math.log2(math.e)
SCALE2 = SCALE * LOG2E
BF = jnp.bfloat16
F32 = jnp.float32
VMEM_LIMIT = 60 << 20


def up128(n):
    return (n + 127) // 128 * 128


def nn(a, b):
    return lax.dot_general(a, b, (((1,), (0,)), ((), ())), preferred_element_type=F32)


def nt(a, b):
    return lax.dot_general(a, b, (((1,), (1,)), ((), ())), preferred_element_type=F32)


def tn(a, b):
    return lax.dot_general(a, b, (((0,), (0,)), ((), ())), preferred_element_type=F32)


def cost(flops, nbytes, trans=0):
    return pl.CostEstimate(flops=int(flops), bytes_accessed=int(nbytes), transcendentals=int(trans))


def params(n_axes):
    sem = ("arbitrary",) * n_axes if n_axes else None
    return pltpu.CompilerParams(dimension_semantics=sem, vmem_limit_bytes=VMEM_LIMIT)


ANY = pl.BlockSpec(memory_space=pl.ANY)
SMEM = pl.BlockSpec(memory_space=pltpu.SMEM)


def all_of(a):
    return pl.BlockSpec(a.shape, lambda *_: (0,) * len(a.shape))


def corner(a):
    last = (min(a.shape[-2], 32 // a.dtype.itemsize), min(a.shape[-1], 128))
    return pl.BlockSpec((1,) * (a.ndim - 2) + last, lambda *_: (0,) * a.ndim)


def run(kernel, operands, specs, waits=(), prefetch=0, **kw):
    n, m = len(operands), len(waits)

    def body(*refs):
        return kernel(*refs[:n], *refs[n + m :])

    grid_spec = pltpu.PrefetchScalarGridSpec(
        num_scalar_prefetch=prefetch,
        grid=kw.pop("grid", (1,)),
        in_specs=[*specs, *[corner(a) for a in waits]],
        out_specs=kw.pop("out_specs"),
        scratch_shapes=kw.pop("scratch_shapes", ()),
    )
    return pl.pallas_call(body, grid_spec=grid_spec, **kw)(*operands, *waits)


class Blocks:
    def __init__(self, heads):
        self.heads = heads
        self.width = up128(heads * (HV + HQ))
        self.vals = heads * HV
        self.k0 = self.vals // 128 * 128
        self.kw = self.width - self.k0

    def stat(self, parts, i):
        return self.vals + i * 3 * (parts + 1)

    def window(self, i):
        wide = max(up128(j * HV % 128 + HV) for j in range(self.heads))
        first = i * HV
        return first, first // 128 * 128, wide


def lanes(shape, start=0):
    return lax.broadcasted_iota(jnp.int32, shape, len(shape) - 1) + start


def row(ref):
    return ref[...].reshape(1, -1)


def take(x, at, first):
    return jnp.sum(jnp.where((at >= first) & (at < first + 3), x, 0.0), axis=1, keepdims=True)


def three_terms(x):
    hi = x.astype(BF).astype(F32)
    mid = (x - hi).astype(BF).astype(F32)
    lo = (x - hi - mid).astype(BF).astype(F32)
    return hi, mid, lo


def norm_kernel(x_ref, g_ref, b_ref, r_ref, xh_ref, s_ref):
    step = min(256, x_ref.shape[1])

    @pl.loop(0, x_ref.shape[1] // step)
    def _(r):
        at = pl.ds(pl.multiple_of(r * step, step), step)
        x = x_ref[0, at, :].astype(F32)
        xc = x - jnp.mean(x, axis=1, keepdims=True)
        rstd = lax.rsqrt(jnp.mean(xc * xc, axis=1, keepdims=True) + EPS)
        xh = xc * rstd
        r_ref[0, at, :] = (xh * row(g_ref) + row(b_ref)).astype(BF)
        xh_ref[0, at, :] = xh.astype(BF)
        s_ref[0, at, :] = jnp.broadcast_to(rstd, (step, s_ref.shape[2]))


def byte_norm(x, g, b):
    seqs, slots, width = x.shape
    tile = min(1024, slots)
    at = lambda s, l: (s, l, 0)
    full = pl.BlockSpec((width,), lambda s, l: (0,))
    return pl.pallas_call(
        norm_kernel,
        grid=(seqs, slots // tile),
        in_specs=[pl.BlockSpec((1, tile, width), at), full, full],
        out_specs=[
            pl.BlockSpec((1, tile, width), at),
            pl.BlockSpec((1, tile, width), at),
            pl.BlockSpec((1, tile, 128), at),
        ],
        out_shape=[
            jax.ShapeDtypeStruct(x.shape, BF),
            jax.ShapeDtypeStruct(x.shape, BF),
            jax.ShapeDtypeStruct((seqs, slots, 128), F32),
        ],
        compiler_params=params(2),
        cost_estimate=cost(10 * x.size, 6 * x.size),
        name="byte_norm",
    )(x, g, b)


def own_latent_kernel(dp_ref, near_ref, far_ref, out_ref, cols):
    dp = dp_ref[0]
    halves = near_ref.shape[0]
    nl, d = out_ref.shape
    dl = d // (2 * halves)
    base = near_ref.shape[1] - dl
    for slot in range(2 * halves):
        src = (far_ref if slot % 2 else near_ref).at[slot // 2]
        cols[pl.ds(pl.multiple_of((dp ^ slot) * dl, 16), dl), :] = src[base:].astype(F32)
    out_ref[...] = cols[...].T[:nl].astype(BF)


def own_latents(nl, d, dp, near, far):
    vm = pl.BlockSpec(memory_space=pltpu.VMEM)
    return pl.pallas_call(
        own_latent_kernel,
        in_specs=[pl.BlockSpec(memory_space=pltpu.SMEM), vm, vm],
        out_specs=vm,
        out_shape=jax.ShapeDtypeStruct((nl, d), BF),
        scratch_shapes=[pltpu.VMEM((d, 128), F32)],
        compiler_params=params(0),
        cost_estimate=cost(nl * d, 8 * nl * d),
        name="own_latents",
    )(dp, near, far)


def latent_kernel(parts, *refs):
    ins, (g_ref, b_ref, out_ref) = refs[:parts], refs[parts:]
    nl = ins[0].shape[0]
    for k in range(parts):
        x = ins[k][...].astype(F32)
        xc = x - jnp.mean(x, axis=1, keepdims=True)
        xh = xc * lax.rsqrt(jnp.mean(xc * xc, axis=1, keepdims=True) + EPS)
        out_ref[k * nl : (k + 1) * nl] = (xh * row(g_ref) + row(b_ref)).astype(BF)


def latent_norm(lats, g, b):
    nl, d = lats[0].shape
    vm = pl.BlockSpec(memory_space=pltpu.VMEM)
    return pl.pallas_call(
        partial(latent_kernel, len(lats)),
        in_specs=[vm] * (len(lats) + 2),
        out_specs=vm,
        out_shape=jax.ShapeDtypeStruct((nl * len(lats), d), BF),
        compiler_params=params(0),
        cost_estimate=cost(10 * nl * len(lats) * d, 4 * nl * len(lats) * d),
        name="latent_norm",
    )(*lats, g, b)


def fwd_kernel(
    blk, parts, tiles, sc_ref, b_ref, near_ref, far_ref, lat_ref, kv_ref, p_ref, y_ref, w_ref, q_ref, wq, acc, cs, st
):
    s = pl.program_id(0)
    n = acc.shape[0]
    nl = n // parts
    slots, width = b_ref.shape[1:]
    d = lat_ref.shape[1]
    me = sc_ref[pl.num_programs(0)]

    @pl.when(s == 0)
    def _():
        dp = sc_ref[pl.num_programs(0) + 1]
        halves = near_ref.shape[0]
        cw, dl = width // (2 * halves), d // (2 * halves)
        for slot in range(2 * halves):
            src = (far_ref if slot % 2 else near_ref).at[slot // 2]
            at = dp ^ slot
            for t in range(tiles):
                w_ref[pl.ds(pl.multiple_of(at * cw, 16), cw), t * 128 : (t + 1) * 128] = src[
                    t * cw : (t + 1) * cw
                ]
            wq[pl.ds(pl.multiple_of(at * dl, 16), dl), :] = src[tiles * cw : tiles * cw + dl]
        q = nn(lat_ref[...], wq[...]).astype(BF).astype(F32)
        at = lanes(q.shape, blk.k0)
        for i in range(blk.heads):
            key = blk.vals + i * HQ
            q_ref[i * n : (i + 1) * n] = jnp.where((at >= key) & (at < key + HQ), q, 0.0).astype(BF)

    kv_ref[0] = nn(b_ref[0], w_ref[...]).astype(BF)

    mask = lanes((n, slots)) < sc_ref[s]
    acc[...] = jnp.zeros_like(acc)
    st[...] = jnp.zeros_like(st)

    for i in range(blk.heads):
        first, start, wide = blk.window(i)
        rows = pl.ds(i * n, n)
        sc = nt(q_ref[rows, :], kv_ref[0, :, blk.k0 :])
        sc = jnp.where(mask, sc, NEGATIVE)
        top = jnp.max(sc, axis=1, keepdims=True)
        p = jnp.exp2((sc - top) * SCALE2)
        total = jnp.sum(p, axis=1, keepdims=True)
        p = (p * (1.0 / total)).astype(BF)
        p_ref[0, rows, :] = p
        o = nn(p, kv_ref[0, :, pl.ds(start, wide)])
        at = lanes((n, wide)) + start
        acc[:, pl.ds(start, wide)] += jnp.where((at >= first) & (at < first + HV), o, 0.0)
        lse = top * SCALE2 + jnp.log(total) * LOG2E
        at = lanes(st.shape, blk.k0)
        for j, term in enumerate(three_terms(lse)):
            st[...] = jnp.where(at == blk.vals + 3 * i + j, term, st[...])

    y = acc[...]
    center = jnp.mean(y, axis=0, keepdims=True).astype(BF).astype(F32)
    y = y - center
    low = (y[:, blk.k0 :] + st[...]).astype(BF)
    y = y.astype(BF)
    for k in range(parts):
        to = pl.ds(pl.multiple_of(s * nl, nl), nl)
        if blk.k0:
            y_ref[me ^ k, to, : blk.k0] = y[k * nl : (k + 1) * nl, : blk.k0]
        y_ref[me ^ k, to, blk.k0 :] = low[k * nl : (k + 1) * nl]
    cs[...] = jnp.where(lax.broadcasted_iota(jnp.int32, cs.shape, 0) == s, center, cs[...])

    @pl.when(s == pl.num_programs(0) - 1)
    def _():
        rows = lax.broadcasted_iota(jnp.int32, cs.shape, 0)
        c = jnp.where(rows < pl.num_programs(0), cs[...], 0.0).astype(BF)
        for k in range(parts):
            y_ref[k, y_ref.shape[1] - 16 :, :] = c


def attend(blk, parts, scalars, bytes_r, near, far, lat_r, waits):
    seqs, slots, width = bytes_r.shape
    n, d = lat_r.shape
    tiles = blk.width // 128
    rows = seqs * (n // parts) + 16
    seq = lambda s, sc: (s, 0, 0)
    flat = lambda s, sc: (0, 0)
    whole = lambda s, sc: (0, 0, 0)
    flops = 2 * seqs * slots * (width * blk.width + blk.heads * n * (blk.kw + 256))
    return run(
        partial(fwd_kernel, blk, parts, tiles),
        (scalars, bytes_r, near, far, lat_r),
        [
            pl.BlockSpec((1, slots, width), seq),
            pl.BlockSpec(near.shape, whole),
            pl.BlockSpec(far.shape, whole),
            pl.BlockSpec(lat_r.shape, flat),
        ],
        waits,
        prefetch=1,
        grid=(seqs,),
        out_specs=[
            pl.BlockSpec((1, slots, blk.width), seq),
            pl.BlockSpec((1, blk.heads * n, slots), seq),
            pl.BlockSpec((parts, rows, blk.width), whole),
            pl.BlockSpec((width, blk.width), flat),
            pl.BlockSpec((blk.heads * n, blk.kw), flat),
            pl.BlockSpec((d, 128), flat),
        ],
        scratch_shapes=[
            pltpu.VMEM((n, blk.width), F32),
            pltpu.VMEM((16, blk.width), F32),
            pltpu.VMEM((n, blk.kw), F32),
        ],
        out_shape=[
            jax.ShapeDtypeStruct((seqs, slots, blk.width), BF),
            jax.ShapeDtypeStruct((seqs, blk.heads * n, slots), BF),
            jax.ShapeDtypeStruct((parts, rows, blk.width), BF),
            jax.ShapeDtypeStruct((width, blk.width), BF),
            jax.ShapeDtypeStruct((blk.heads * n, blk.kw), BF),
            jax.ShapeDtypeStruct((d, 128), BF),
        ],
        compiler_params=params(1),
        cost_estimate=cost(flops, 4 * seqs * slots * width, seqs * blk.heads * n * slots),
        name="attend_forward",
    )


def rows_kernel(blk, parts, seqs, order, *refs):
    me_ref, *refs = refs
    pays, refs = refs[:parts], refs[parts:]
    lat_ref, cot_ref, g_ref, b_ref, bh_ref, bb_ref, w_hbm = refs[:7]
    outs, refs = refs[7 : 7 + len(order)], refs[7 + len(order) :]
    out_ref, lx_ref, rx_ref, lm_ref, rm_ref, vec_ref, dsum_ref = refs[:7]
    w_ref, mix, st, mid_s, acc, pay_ref, dbh, sums, total_s, sems = refs[7:]
    me = me_ref[0]
    rows, d = acc.shape
    nl = rows // seqs
    ff = w_hbm.shape[2]
    fw = blk.vals
    back0 = fw // 128 * 128
    shift = fw - back0
    back = slice(back0, back0 + blk.width)
    out0 = up128(2 * fw)
    wide = slice(0, blk.width)
    low = slice(out0, out0 + blk.width)

    def copies():
        for t in range(parts):
            yield pltpu.make_async_copy(w_hbm.at[t], w_ref.at[t], sems.at[0])

    for c in copies():
        c.start()
    @pl.loop(0, seqs)
    def _(s):
        sl = pl.ds(pl.multiple_of(s * nl, nl), nl)
        for j in range(parts):
            ys = [pays[k ^ j][me ^ k, sl, :].astype(F32) for k in range(parts)]
            at = lanes((nl, blk.kw), blk.k0)
            stat = jnp.zeros((nl, blk.kw), F32)
            weights = []
            for i in range(blk.heads):
                lse = [take(y[:, blk.k0 :], at, blk.vals + 3 * i) for y in ys]
                top = lse[0]
                for x in lse[1:]:
                    top = jnp.maximum(top, x)
                es = [jnp.exp2(x - top) for x in lse]
                total = sum(es[1:], es[0])
                weights.append([e / total for e in es])
                for k in range(parts):
                    for q, term in enumerate(three_terms(weights[i][k])):
                        stat = jnp.where(at == blk.stat(parts, i) + 3 * k + q, term, stat)
            st[j, sl, :] = stat
            at = lanes((nl, blk.width))
            pick = (lax.broadcasted_iota(jnp.int32, (nl, 16), 1) == s).astype(BF)
            m = jnp.zeros((nl, blk.width), F32)
            for k in range(parts):
                wt = jnp.zeros((nl, blk.width), F32)
                for i in range(blk.heads):
                    wt = jnp.where((at >= i * HV) & (at < (i + 1) * HV), weights[i][k], wt)
                m = m + (ys[k] + nn(pick, pays[k ^ j][me ^ k, seqs * nl :, :])) * wt
            m = jnp.where(at < blk.vals, m, 0.0)
            mix[j, sl, :] = m
            rm_ref[j, sl, :] = m.astype(BF)

    for c in copies():
        c.wait()

    acc[...] = jnp.zeros_like(acc)

    @pl.loop(0, parts)
    def _(j):
        acc[...] += nt(rm_ref[j], w_ref[me ^ j, :, low])

    def centred(x):
        xc = x - jnp.mean(x, axis=1, keepdims=True)
        rstd = lax.rsqrt(jnp.mean(xc * xc, axis=1, keepdims=True) + EPS)
        return xc * rstd, rstd

    @pl.loop(0, seqs)
    def _(s):
        sl = pl.ds(pl.multiple_of(s * nl, nl), nl)
        mid = acc[sl, :] + lat_ref[...].astype(F32)
        mid_s[sl, :] = mid
        lx_ref[0, sl, :] = (centred(mid)[0] * row(g_ref) + row(b_ref)).astype(BF)
        lx_ref[1, sl, :] = cot_ref[sl, :].astype(BF)
        out_ref[sl, :] = mid + row(bb_ref)
        acc[sl, :] = jnp.zeros((nl, d), F32)

    @pl.loop(0, parts)
    def _(j):
        t = me ^ j
        live = lanes((rows, blk.width)) < fw
        pre = nn(lx_ref[0], w_ref[t, :, wide]) + bh_ref[t]
        phi = 0.5 * (1.0 + lax.erf(pre * math.sqrt(0.5)))
        slope = phi + pre * (jnp.exp(-0.5 * pre * pre) * (1.0 / math.sqrt(2.0 * math.pi)))
        act = jnp.where(live, pre * phi, 0.0)
        rx_ref[1, j] = (pltpu.roll(act, shift, 1) if shift else act).astype(BF)
        dact = nn(lx_ref[1], w_ref[t, :, back])
        dact = pltpu.roll(dact, blk.width - shift, 1) if shift else dact
        dpre = jnp.where(live, dact * slope, 0.0).astype(BF)
        rx_ref[0, j] = dpre
        dbh[t] = jnp.sum(dpre.astype(F32), axis=0, keepdims=True)
        out_ref[...] += nt(rx_ref[1, j], w_ref[t, :, back])
        acc[...] += nt(rx_ref[0, j], w_ref[t, :, wide])

    sums[...] = jnp.zeros_like(sums)
    total_s[...] = jnp.zeros_like(total_s)

    @pl.loop(0, seqs)
    def _(s):
        sl = pl.ds(pl.multiple_of(s * nl, nl), nl)
        xh, rstd = centred(mid_s[sl, :])
        dy, cot = acc[sl, :], cot_ref[sl, :]
        for i, v in enumerate((dy * xh, dy, cot)):
            sums[i : i + 1] += jnp.sum(v, axis=0, keepdims=True)
        e = dy * row(g_ref)
        dv = rstd * (
            e - jnp.mean(e, axis=1, keepdims=True) - xh * jnp.mean(e * xh, axis=1, keepdims=True)
        )
        dmid = cot + dv
        lm_ref[sl, :] = dmid.astype(BF)
        total_s[...] += dmid

    dsum_ref[...] = total_s[...].astype(BF)
    cuts = d // 128
    for i in range(3):
        for c in range(cuts):
            vec_ref[i * cuts + c : i * cuts + c + 1] = sums[i : i + 1, c * 128 : (c + 1) * 128]
    vec_ref[3 * cuts :] = jnp.zeros((vec_ref.shape[0] - 3 * cuts, 128), F32)
    for t in range(parts):
        first, move = t * fw // 128, t * fw % 128
        v = jnp.concatenate([dbh[t], jnp.zeros((1, 128), F32)], axis=1)
        v = pltpu.roll(v, move, 1) if move else v
        for c in range(v.shape[1] // 128):
            if first + c < cuts:
                vec_ref[3 * cuts + first + c : 3 * cuts + first + c + 1] += v[:, c * 128 : (c + 1) * 128]

    @pl.loop(0, parts)
    def _(j):
        dm = nn(lm_ref[...], w_ref[me ^ j, :, low]).astype(BF)
        prod = dm.astype(F32) * mix[j]
        at = lanes(prod.shape)
        stat = st[j]
        at_k = lanes(stat.shape, blk.k0)
        for i in range(blk.heads):
            inner = jnp.sum(
                jnp.where((at >= i * HV) & (at < (i + 1) * HV), prod, 0.0), axis=1, keepdims=True
            )
            for q, term in enumerate(three_terms(inner)):
                stat = jnp.where(at_k == blk.stat(parts, i) + 3 * parts + q, term, stat)
        if blk.k0:
            pay_ref[j, :, : blk.k0] = dm[:, : blk.k0]
        pay_ref[j, :, blk.k0 :] = jnp.where(at_k < blk.vals, dm[:, blk.k0 :].astype(F32), stat).astype(BF)

    for out, stages in zip(outs, order, strict=True):
        for i, stage in enumerate(stages):
            for k in range(parts):
                out[me ^ k, i] = pay_ref[stage ^ k]


def rows_step(blk, parts, seqs, order, me, pays, lat, cot, g, b, bh, bb, w):
    rows, d = cot.shape
    nl = rows // seqs
    whole = lambda a: pl.BlockSpec(a.shape, lambda i, me, r=len(a.shape): (0,) * r)
    outs = [jax.ShapeDtypeStruct((parts, len(o), rows, blk.width), BF) for o in order] + [
        jax.ShapeDtypeStruct((rows, d), F32),
        jax.ShapeDtypeStruct((2, rows, d), BF),
        jax.ShapeDtypeStruct((2, parts, rows, blk.width), BF),
        jax.ShapeDtypeStruct((rows, d), BF),
        jax.ShapeDtypeStruct((parts, rows, blk.width), BF),
        jax.ShapeDtypeStruct(((4 * d // 128 + 7) // 8 * 8, 128), F32),
        jax.ShapeDtypeStruct((nl, d), BF),
    ]
    return pl.pallas_call(
        partial(rows_kernel, blk, parts, seqs, order),
        grid_spec=pltpu.PrefetchScalarGridSpec(
            num_scalar_prefetch=1,
            grid=(1,),
            in_specs=[whole(a) for a in pays]
            + [whole(a) for a in (lat, cot, g, b, bh, bb)]
            + [ANY],
            out_specs=[whole(o) for o in outs],
            scratch_shapes=[
                pltpu.VMEM((parts, d, w.shape[-1]), BF),
                pltpu.VMEM((parts, rows, blk.width), F32),
                pltpu.VMEM((parts, rows, blk.kw), F32),
                pltpu.VMEM((rows, d), F32),
                pltpu.VMEM((rows, d), F32),
                pltpu.VMEM((parts, rows, blk.width), BF),
                pltpu.VMEM((parts, 1, blk.width), F32),
                pltpu.VMEM((8, d), F32),
                pltpu.VMEM((nl, d), F32),
                pltpu.SemaphoreType.DMA((1,)),
            ],
        ),
        out_shape=outs,
        compiler_params=params(1),
        cost_estimate=cost(12 * rows * d * d, 2 * w.size + 40 * rows * d, 2 * rows * d),
        name="rows",
    )(me, *pays, lat, cot, g, b, bh, bb, w)


def ff_kernel(blk, me_ref, lh_ref, lo_ref, rd_ref, ra_ref, out_ref):
    fw = blk.vals
    back0 = fw // 128 * 128
    hid = tn(lh_ref[0], rd_ref[0, 0])
    back = tn(lo_ref[0], ra_ref[0, 0])
    dps, _, dl, wide = out_ref.shape
    cuts = [(0, back0, hid[:, :back0])] if back0 else []
    if back0 < blk.width:
        n = blk.width - back0
        cuts.append((back0, n, hid[:, back0:] + back[:, :n]))
        cuts.append((blk.width, wide - blk.width, back[:, n : n + wide - blk.width]))
    for at, n, piece in cuts:
        if n:
            out_ref[:, 0, :, at : at + n] = piece.astype(BF).reshape(dps, dl, n)


def ff_grads(blk, me, dps, lx, rx):
    _, parts, rows, width = rx.shape
    d = lx.shape[2]
    wide = up128(2 * blk.vals)
    return pl.pallas_call(
        partial(ff_kernel, blk),
        grid_spec=pltpu.PrefetchScalarGridSpec(
            num_scalar_prefetch=1,
            grid=(parts,),
            in_specs=[
                pl.BlockSpec((1, rows, d), lambda i, me: (0, 0, 0)),
                pl.BlockSpec((1, rows, d), lambda i, me: (1, 0, 0)),
                pl.BlockSpec((1, 1, rows, width), lambda i, me: (0, i, 0, 0)),
                pl.BlockSpec((1, 1, rows, width), lambda i, me: (1, i, 0, 0)),
            ],
            out_specs=pl.BlockSpec((dps, 1, d // dps, wide), lambda i, me: (0, me[0] ^ i, 0, 0)),
        ),
        out_shape=jax.ShapeDtypeStruct((dps, parts, d // dps, wide), BF),
        compiler_params=params(1),
        cost_estimate=cost(4 * parts * rows * d * width, 4 * parts * d * width),
        name="ff_grads",
    )(me, lx, lx, rx, rx)


def slot_place(slot, dps):
    return (slot & 1) * (dps // 2) + (slot >> 1)


def core_slot(core, i, half):
    return core * half + ((i ^ (1 - core)) if half > 1 else i)


def out_kernel(half, dps, sc_ref, lx_ref, rx_ref, lx2_ref, rx2_ref, *outs):
    core, dp = sc_ref[0], sc_ref[1]
    dl = lx_ref.shape[1] // dps
    for i, out_ref in enumerate(outs):
        slot = core_slot(core, i, half)
        r = (tn(lx_ref[...], rx_ref[slot]) + tn(lx2_ref[...], rx2_ref[slot])).astype(BF)
        for z in range(dps):
            out_ref[slot_place(dp ^ z, dps)] = r[z * dl : (z + 1) * dl]


def out_grads(scalars, dps, lx, rx, lx2, rx2, waits):
    parts, rows, width = rx.shape
    d = lx.shape[1]
    half = max(parts // 2, 1)
    whole = lambda a: pl.BlockSpec(a.shape, lambda i, sc, r=len(a.shape): (0,) * r)
    outs = [jax.ShapeDtypeStruct((dps, d // dps, width), BF)] * half
    return run(
        partial(out_kernel, half, dps),
        (scalars, lx, rx, lx2, rx2),
        [whole(a) for a in (lx, rx, lx2, rx2)],
        waits,
        prefetch=1,
        out_specs=[whole(o) for o in outs],
        out_shape=outs,
        compiler_params=params(1),
        cost_estimate=cost(4 * half * rows * d * width, 2 * half * d * width),
        name="out_grads",
    )


def bwd_kernel(blk, parts, dps, count, add, sc_ref, *refs):
    kvs, ps, qs, ws, refs = (
        refs[:count],
        refs[count : 2 * count],
        refs[2 * count : 3 * count],
        refs[3 * count : 4 * count],
        refs[4 * count :],
    )
    xh_ref, g_ref, b_ref, dm_ref, *refs = refs
    extra, refs = refs[:add], refs[add:]
    dkvs, gws, refs = refs[:count], refs[count : 2 * count], refs[2 * count :]
    dq_ref, dgb_ref, dkvt, gacc, sacc, dmx, dqs, dqg = refs
    me, dp = sc_ref[0], sc_ref[1]
    s = pl.program_id(0)
    n = dmx.shape[1]
    nl = n // parts
    off, qk = blk.vals - blk.k0, blk.heads * HQ

    @pl.when(s == 0)
    def _():
        gacc[...] = jnp.zeros_like(gacc)
        sacc[...] = jnp.zeros_like(sacc)
        dqs[...] = jnp.zeros_like(dqs)

    for c in range(count):
        kv_ref, p_ref = kvs[c], ps[c]
        for k in range(parts):
            dmx[c, k * nl : (k + 1) * nl] = dm_ref[me ^ k, c]
        tail = dmx[c, :, blk.k0 :].astype(F32)
        at_k = lanes(tail.shape, blk.k0)
        at_n = lax.broadcasted_iota(jnp.int32, (n, 1), 0)
        dkvt[c] = jnp.zeros_like(dkvt[c])
        for i in range(blk.heads):
            first, start, width = blk.window(i)
            rows = pl.ds(i * n, n)
            cols = pl.ds(start, width)
            stat = blk.stat(parts, i)
            ratio = take(tail, at_k, stat)
            for k in range(1, parts):
                ratio = jnp.where(at_n >= k * nl, take(tail, at_k, stat + 3 * k), ratio)
            inner = take(tail, at_k, stat + 3 * parts)
            at = lanes((n, width)) + start
            dm = dmx[c, :, cols].astype(F32)
            dm = jnp.where((at >= first) & (at < first + HV), dm, 0.0)
            dpr = nt(dm.astype(BF), kv_ref[0, :, cols])
            ds = (p_ref[0, rows, :].astype(F32) * ((dpr - inner) * (ratio * SCALE))).astype(BF)
            dkvt[c, cols, :] += tn((dm * ratio).astype(BF), p_ref[0, rows, :])
            dkvt[c, blk.k0 :, :] += tn(qs[c][rows, :], ds)
            dq = nn(ds, kv_ref[0, :, blk.k0 :])
            key = blk.vals + i * HQ
            dqs[c] += jnp.where((at_k >= key) & (at_k < key + HQ), dq, 0.0)

        low = dkvt[c].astype(BF)
        dkvs[c][0] = low.T
        gacc[c] += nn(low, xh_ref[0])
        sacc[c] += jnp.sum(low.astype(F32), axis=1, keepdims=True)

    @pl.when(s == pl.num_programs(0) - 1)
    def _():
        dg, db = 0.0, 0.0
        for c in range(count):
            wt = ws[c][...].T.astype(F32)
            grad, col = gacc[c], sacc[c, :, 0:1]
            dg = dg + jnp.sum(wt * grad, axis=0, keepdims=True)
            db = db + jnp.sum(wt * col, axis=0, keepdims=True)
            gw = (grad * row(g_ref) + col * row(b_ref)).T.astype(BF)
            cl = gw.shape[0] // dps
            for z in range(dps):
                gws[c][slot_place(dp ^ z, dps), :cl] = gw[z * cl : (z + 1) * cl]
            if add and c == count - 1:
                more = jnp.where(dp % 2 == 0, extra[0][...].astype(F32), 0.0)
                for e in extra[1:]:
                    more = more + e[...].astype(F32)
                gws[c][:, cl:] = more.astype(BF)
            for k in range(parts):
                dqg[pl.ds(pl.multiple_of((me ^ k) * nl, 8), nl), :] = dqs[c, k * nl : (k + 1) * nl]
            left = pltpu.roll(dqg[: n // 2], (128 - off) % 128, 1)
            right = pltpu.roll(dqg[n // 2 :], (64 - off) % 128, 1)
            dq_ref[c] = left + right
        cuts = dg.shape[1] // 128
        dgb_ref[...] = jnp.zeros_like(dgb_ref)
        for i, v in enumerate((dg, db)):
            for c in range(cuts):
                dgb_ref[i * cuts + c : i * cuts + c + 1] = v[:, c * 128 : (c + 1) * 128]


def attend_backward(blk, parts, dps, scalars, kvs, ps, qs, ws, xh, g, b, pay, extra, waits):
    seqs, slots, width = xh.shape
    count = len(kvs)
    n = qs[0].shape[0] // blk.heads
    nl = n // parts
    seq = lambda s, sc: (s, 0, 0)
    cl = width // dps
    sizes = [cl] * count
    if extra:
        sizes[-1] += extra[0].shape[1]
    outs = (
        [jax.ShapeDtypeStruct((seqs, slots, blk.width), BF)] * count
        + [jax.ShapeDtypeStruct((dps, r, blk.width), BF) for r in sizes]
        + [
            jax.ShapeDtypeStruct((count, n // 2, 128), F32),
            jax.ShapeDtypeStruct(((2 * width // 128 + 7) // 8 * 8, 128), F32),
        ]
    )
    res = run(
        partial(bwd_kernel, blk, parts, dps, count, len(extra)),
        (scalars, *kvs, *ps, *qs, *ws, xh, g, b, pay, *extra),
        [pl.BlockSpec((1, slots, blk.width), seq)] * count
        + [pl.BlockSpec((1, blk.heads * n, slots), seq)] * count
        + [all_of(a) for a in (*qs, *ws)]
        + [
            pl.BlockSpec((1, slots, width), seq),
            all_of(g),
            all_of(b),
            pl.BlockSpec((parts, count, nl, blk.width), lambda s, sc: (0, 0, s, 0)),
        ]
        + [all_of(a) for a in extra],
        waits,
        prefetch=1,
        grid=(seqs,),
        out_specs=[pl.BlockSpec((1, slots, blk.width), seq)] * count + [all_of(o) for o in outs[count:]],
        scratch_shapes=[
            pltpu.VMEM((count, blk.width, slots), F32),
            pltpu.VMEM((count, blk.width, width), F32),
            pltpu.VMEM((count, blk.width, 128), F32),
            pltpu.VMEM((count, n, blk.width), BF),
            pltpu.VMEM((count, n, blk.kw), F32),
            pltpu.VMEM((n, blk.kw), F32),
        ],
        out_shape=outs,
        compiler_params=params(1),
        cost_estimate=cost(
            2 * count * seqs * slots * (width * blk.width + 4 * blk.heads * n * 256),
            (2 + 4 * count) * seqs * slots * width,
        ),
        name="attend_backward",
    )
    return res[:count], res[count : 2 * count], res[2 * count], res[2 * count + 1]


def bytes_kernel(parts, *refs):
    dkvs, ws = refs[:parts], refs[parts : 2 * parts]
    xh_ref, s_ref, g_ref, *_, out_ref, done_ref = refs[2 * parts :]
    done_ref[...] = jnp.zeros_like(done_ref)
    step = min(256, out_ref.shape[1])

    @pl.loop(0, out_ref.shape[1] // step)
    def _(r):
        at = pl.ds(pl.multiple_of(r * step, step), step)
        dy = nt(dkvs[0][0, at, :], ws[0][...])
        for k in range(1, parts):
            dy = dy + nt(dkvs[k][0, at, :], ws[k][...])
        xh = xh_ref[0, at, :].astype(F32)
        e = dy * row(g_ref)
        me = jnp.mean(e, axis=1, keepdims=True)
        mx = jnp.mean(e * xh, axis=1, keepdims=True)
        out_ref[0, at, :] = s_ref[0, at, 0:1] * (e - me - xh * mx)


def byte_grads(s, dkvs, ws, xh, rstd, g, into, waits):
    _, slots, width = xh.shape
    bw = ws[0].shape[1]
    tile = min(512, slots)
    at = lambda l: (s, l, 0)
    flat = lambda l: (0, 0)
    kept = [] if into is None else [into]
    return run(
        partial(bytes_kernel, len(ws)),
        (*dkvs, *ws, xh, rstd, g, *kept),
        [pl.BlockSpec((1, tile, bw), at) for _ in dkvs]
        + [pl.BlockSpec((width, bw), flat) for _ in ws]
        + [
            pl.BlockSpec((1, tile, width), at),
            pl.BlockSpec((1, tile, 128), at),
            all_of(g),
        ]
        + [ANY] * len(kept),
        waits,
        grid=(slots // tile,),
        out_specs=[pl.BlockSpec((1, tile, width), at), pl.BlockSpec((8, 128), flat)],
        out_shape=[jax.ShapeDtypeStruct(xh.shape, F32), jax.ShapeDtypeStruct((8, 128), BF)],
        input_output_aliases={2 * len(ws) + 3: 0} if kept else {},
        compiler_params=params(1),
        cost_estimate=cost(2 * slots * width * bw * len(ws), 10 * slots * width),
        name="byte_grads",
    )


def latent_back_kernel(parts, dps, off, sizes, sc_ref, msg_ref, *refs):
    lat_refs, lqs, (g_ref, b_ref), refs = (
        refs[:parts],
        refs[parts : 2 * parts],
        refs[2 * parts : 2 * parts + 2],
        refs[2 * parts + 2 :],
    )
    gq_ref, dv_ref, sg_ref, sb_ref, *vecs = refs[:-3]
    dys, tr, dqx = refs[-3:]
    me, dp = sc_ref[0], sc_ref[1]
    nl, d = lat_refs[0].shape
    n = nl * parts
    h = n // 2
    dl = d // dps
    at = lanes((h, 128))
    dys[...] = jnp.zeros_like(dys)
    for k in reversed(range(parts)):
        both = msg_ref[k * h : (k + 1) * h]
        dqx[:h] = pltpu.roll(jnp.where(at < 64, both, 0.0), off, 1)
        dqx[h:] = pltpu.roll(jnp.where(at >= 64, both, 0.0), (off + 64) % 128, 1)
        dys[...] += nt(dqx[...].astype(BF), lqs[k][...])
    g, b = row(g_ref), row(b_ref)
    dg, db = jnp.zeros((1, d), F32), jnp.zeros((1, d), F32)
    for k in range(parts):
        rows = pl.ds(pl.multiple_of((me ^ k) * nl, 8), nl)
        x = lat_refs[k][...].astype(F32)
        xc = x - jnp.mean(x, axis=1, keepdims=True)
        rs = lax.rsqrt(jnp.mean(xc * xc, axis=1, keepdims=True) + EPS)
        xh = xc * rs
        dy = dys[rows, :]
        dg = dg + jnp.sum(dy * xh, axis=0, keepdims=True)
        db = db + jnp.sum(dy, axis=0, keepdims=True)
        if k == 0:
            e = dy * g
            keep = rs * (
                e - jnp.mean(e, axis=1, keepdims=True) - xh * jnp.mean(e * xh, axis=1, keepdims=True)
            )
        dys[rows, :] = xh * g + b
    sg_ref[...] = dg[0]
    sb_ref[...] = db[0]
    tr[...] = dys[...].T
    mine = tr[pl.ds(pl.multiple_of(dp * dl, 8), dl), :].astype(BF)
    gq_ref[...] = nn(mine, dqx[...].astype(BF))
    tr[:, :nl] = keep.T
    dv_ref[...] = tr[pl.ds(pl.multiple_of(dp * dl, 8), dl), :nl]
    first = parts * h
    for ref, start, size in zip(vecs, *sizes, strict=True):
        for c in range(size // 128):
            ref[c * 128 : (c + 1) * 128] = msg_ref[first + start + c : first + start + c + 1].reshape(128)


def latent_back(dps, off, starts, sizes, scalars, msg, lats, lqs, g, b):
    parts = len(lats)
    nl, d = lats[0].shape
    n = nl * parts
    vm = pl.BlockSpec(memory_space=pltpu.VMEM)
    return pl.pallas_call(
        partial(latent_back_kernel, parts, dps, off, (starts, sizes)),
        in_specs=[SMEM] + [vm] * (2 * parts + 3),
        out_specs=[vm] * (4 + len(sizes)),
        out_shape=[
            jax.ShapeDtypeStruct((d // dps, 128), F32),
            jax.ShapeDtypeStruct((d // dps, nl), F32),
            jax.ShapeDtypeStruct((d,), F32),
            jax.ShapeDtypeStruct((d,), F32),
        ]
        + [jax.ShapeDtypeStruct((s,), F32) for s in sizes],
        scratch_shapes=[pltpu.VMEM((n, d), F32), pltpu.VMEM((d, n), F32), pltpu.VMEM((n, 128), F32)],
        compiler_params=params(0),
        cost_estimate=cost(2 * n * 128 * d * parts, 10 * d * n),
        name="latent_back",
    )(scalars, msg, *lats, *lqs, g, b)


def on_device(
    dps,
    parts,
    byte_in,
    lengths,
    latent,
    g_in,
    b_in,
    g_lat,
    b_lat,
    w_query,
    w_key,
    w_value,
    w_out,
    g_mlp,
    b_mlp,
    w_hidden,
    b_hidden,
    w_back,
    b_back,
    cotangent,
):
    seqs, slots, width = byte_in.shape
    nl, dl = latent.shape
    n, d = nl * parts, dl * dps
    blk = Blocks(w_key.shape[1] // HQ)
    qk = w_key.shape[1]
    bw = blk.width
    me = lax.axis_index("tensor").astype(jnp.int32)
    dp = lax.axis_index("dp").astype(jnp.int32)
    core = dp % 2

    def hop(x, k):
        return lax.ppermute(x, "tensor", [(i, i ^ k) for i in range(parts)])

    def hop_dp(x, k):
        return lax.ppermute(x, "dp", [(i, i ^ k) for i in range(dps)])

    def swap(x):
        return lax.all_to_all(x, "tensor", split_axis=0, concat_axis=0, tiled=True)

    def widen(x):
        return jnp.pad(x, ((0, 0), (0, bw - x.shape[1])))

    def after(x, *others):
        return lax.optimization_barrier((x, *others))[0]

    fw = d // parts
    mats = jnp.concatenate([w_hidden, w_back.T], axis=1)
    mats = jnp.pad(mats, ((0, 0), (0, up128(2 * fw) - 2 * fw)))
    mats = jnp.concatenate([mats, widen(w_out.T)], axis=1)

    tiles = bw // 128
    off = blk.vals - blk.k0
    dp1, me1 = dp.reshape(1), me.reshape(1)
    shard = widen(jnp.concatenate([w_value, w_key], axis=1))
    lq = jnp.concatenate([jnp.pad(latent.T, ((0, 0), (0, off - nl))), w_query], axis=1)
    lq = jnp.pad(lq, ((0, 0), (0, 128 - off - qk)))
    shard = jnp.concatenate([shard[:, t * 128 : (t + 1) * 128] for t in range(tiles)] + [lq], axis=0)
    got = [hop_dp(shard, j) for j in range(2, dps, 2)]
    bytes_r, xh, rstd = byte_norm(after(byte_in, shard), g_in, b_in)
    near = after(jnp.stack([shard] + got, axis=0), rstd)
    far = hop_dp(near, 1)
    lat = own_latents(nl, d, dp1, near, far)
    lats = [lat] + [hop(lat, k) for k in range(1, parts)]
    lat_r = latent_norm(lats, g_lat, b_lat)
    gate = lax.optimization_barrier((near, far, *lats))
    nears = [near] + [hop(gate[0], k) for k in range(1, parts)]
    fars = [far]
    mats = lax.all_gather(after(mats, gate[0]), ("tensor", "dp"), axis=0, tiled=True).reshape(parts, d, -1)

    live = jnp.clip(lengths - me * slots, 0, slots).astype(jnp.int32)
    scalars = jnp.concatenate([live, me1, dp1])
    kvs, ps, ws, qs, lqs, pays = [], [], [], [], [], []
    for k in range(parts):
        waits = []
        if k == 1:
            late = lax.optimization_barrier((kvs[0], *nears[1:]))[1:]
            fars += [hop_dp(a, 1) for a in late]
        if k:
            waits.append(kvs[k - 1])
        if k > 1:
            waits.append(pays[k - 2])
        kv, p, y, w, q, lq = attend(blk, parts, scalars, bytes_r, nears[k], fars[k], lat_r, waits)
        kvs.append(kv)
        ps.append(p)
        ws.append(w)
        qs.append(q)
        lqs.append(lq)
        pays.append(swap(y))

    rows = seqs * nl
    bh = jnp.pad(b_hidden.reshape(parts, 1, -1), ((0, 0), (0, 0), (0, bw - fw)))
    slots_left = list(range(1, parts)) + [0]
    order = [slots_left[i : i + 2] for i in range(0, parts, 2)]
    res = rows_step(
        blk,
        parts,
        seqs,
        order,
        jnp.stack([me, core]),
        pays,
        lat,
        cotangent.reshape(rows, d),
        g_mlp,
        b_mlp,
        bh,
        b_back,
        mats,
    )
    dpays, (out, lx, rx, lm, rm, vec_rows, dsum) = res[: len(order)], res[len(order) :]
    latents_out = out.reshape(seqs, nl, d)
    dpays = [swap(a) for a in dpays]
    lm2, rm2 = hop_dp(lm, 1), hop_dp(rm, 1)
    ff = ff_grads(blk, me1, dps, lx, rx)
    scalars = jnp.stack([me, dp])
    pairs = out_grads(jnp.stack([core, dp]), dps, lm, rm, lm2, rm2, [ff])
    half = len(pairs)
    moved = []
    for i in range(half):
        perm = []
        for z in range(dps):
            for t in range(parts):
                c = z % 2
                slot = c * half + ((i ^ (1 - c)) if half > 1 else i)
                if slot:
                    perm.append((z * parts + t, z * parts + (t ^ slot)))
        moved.append(lax.ppermute(pairs[i], ("dp", "tensor"), perm))
    ff = lax.psum_scatter(ff, "dp", scatter_dimension=0, tiled=True).reshape(parts, dl, -1)
    grad_sum = lax.psum_scatter(dsum, "dp", scatter_dimension=1, tiled=True).astype(F32)

    dkvs, dqs, gws, dgb = [None] * parts, [None] * parts, [None] * parts, None
    for at, ks in enumerate(order):
        last = at == len(order) - 1
        got, grads, dq, dgb_k = attend_backward(
            blk,
            parts,
            dps,
            scalars,
            [kvs[k] for k in ks],
            [ps[k] for k in ks],
            [qs[k] for k in ks],
            [ws[k] for k in ks],
            xh,
            g_in,
            b_in,
            dpays[at],
            [pairs[min(1, half - 1)], *moved] if last else [],
            [pairs[0]] if at == 0 else [],
        )
        for i, k in enumerate(ks):
            dkvs[k], dqs[k] = got[i], dq[i]
            gws[k] = hop(grads[i], k) if k else grads[i]
        dgb = dgb_k if dgb is None else dgb + dgb_k

    cl = width // dps
    head = n // 2

    def blocks_of(msg, j):
        if not j:
            return msg
        return jnp.concatenate(
            [msg[(k ^ j) * head : ((k ^ j) + 1) * head] for k in range(parts)] + [msg[parts * head :]], axis=0
        )

    msg = jnp.concatenate([*dqs, dgb, vec_rows], axis=0)
    steps, j = [], 2
    while j < dps:
        steps.insert(0, (hop_dp, j, 0))
        j *= 2
    j = 1
    while j < parts:
        steps.insert(1, (hop, j, j))
        j *= 2
    steps.insert(0, (hop_dp, 1, 0))
    h = dps // 2
    grad_bytes = None
    todo = list(range(seqs))

    def cover(waits, *values):
        nonlocal grad_bytes
        if todo:
            grad_bytes, done = byte_grads(todo.pop(0), dkvs, ws, xh, rstd, g_in, grad_bytes, waits)
            values = lax.optimization_barrier((done, *values))[1:]
        return values

    def step(msg):
        f, j, slot = steps.pop(0)
        return msg + blocks_of(f(msg, j), slot)

    msg = step(msg)
    ready, msg = msg, step(msg)
    msg, *late = cover((ready,), msg, *[gws[k] for k in order[-1] if k])
    others = sum(gws[k].astype(F32) for ks in order[:-1] for k in ks) + sum(g.astype(F32) for g in late)
    total = jnp.concatenate([gws[0][:, :cl].astype(F32) + others, gws[0][:, cl:].astype(F32)], axis=1).astype(BF)
    sums = total[:h].astype(F32) + hop_dp(total[h:], 1).astype(F32)
    ready, msg = msg, step(msg)
    low = sums.astype(BF)
    (msg, low) = cover((ready, total), msg, low)
    got = [hop_dp(low[z], 2 * z) for z in range(1, h)]
    waits = [low]
    while steps:
        ready, msg = msg, step(msg)
        (msg,) = cover((ready, *waits), msg)
        waits = got
    while todo:
        cover((msg,), msg)
    total = sums[0] + sum(g.astype(F32) for g in got)
    grad_kv, grad_out = total[:cl], total[cl:, :fw]
    ff = jnp.sum(swap(ff).astype(F32), axis=0)

    wide, long = width // 128, d // 128
    first = dgb.shape[0]
    starts = [0, wide, first, first + long, first + 2 * long, first + 3 * long]
    gq, dv, sum_g_lat, sum_b_lat, sum_g_in, sum_b_in, sum_g_mlp, sum_b_mlp, sum_back, sum_hidden = latent_back(
        dps, off, starts, [width, width, d, d, d, d], scalars, msg, lats, lqs, g_lat, b_lat
    )
    grad_latent = grad_sum + dv.T

    return (
        latents_out,
        grad_bytes,
        grad_latent,
        sum_g_in,
        sum_b_in,
        sum_g_lat,
        sum_b_lat,
        gq[:, off : off + qk],
        grad_kv[:, blk.vals : blk.vals + qk],
        grad_kv[:, : blk.vals],
        grad_out.T,
        sum_g_mlp,
        sum_b_mlp,
        ff[:, :fw],
        sum_hidden,
        ff[:, fw : 2 * fw].T,
        sum_back,
    )


def solution(mesh):
    return jax.shard_map(
        partial(on_device, mesh.shape["dp"], mesh.shape["tensor"]),
        mesh=mesh,
        in_specs=(
            P("dp", "tensor", None),
            P("dp"),
            P("tensor", "dp"),
            P(),
            P(),
            P(),
            P(),
            P("dp", "tensor"),
            P("dp", "tensor"),
            P("dp", "tensor"),
            P("tensor", "dp"),
            P(),
            P(),
            P("dp", "tensor"),
            P(),
            P("tensor", "dp"),
            P(),
            P("dp", "tensor", None),
        ),
        out_specs=(
            P("dp", "tensor", None),
            P("dp", "tensor", None),
            P("tensor", "dp"),
            P(),
            P(),
            P(),
            P(),
            P("dp", "tensor"),
            P("dp", "tensor"),
            P("dp", "tensor"),
            P("tensor", "dp"),
            P(),
            P(),
            P("dp", "tensor"),
            P(),
            P("tensor", "dp"),
            P(),
        ),
        check_vma=False,
    )
```

```python
from functools import partial
import math

import jax
import jax.numpy as jnp
from jax import lax
from jax.experimental import pallas as pl
from jax.experimental.pallas import tpu as pltpu
from jax.sharding import PartitionSpec as P

HQ = 32
HV = 160
EPS = 1e-05
NEGATIVE = -1e30
SCALE = HQ**-0.5
LOG2E = math.log2(math.e)
SCALE2 = SCALE * LOG2E
BF = jnp.bfloat16
F32 = jnp.float32
VMEM_LIMIT = 60 << 20


def up128(n):
    return (n + 127) // 128 * 128


def nn(a, b):
    return lax.dot_general(a, b, (((1,), (0,)), ((), ())), preferred_element_type=F32)


def nt(a, b):
    return lax.dot_general(a, b, (((1,), (1,)), ((), ())), preferred_element_type=F32)


def tn(a, b):
    return lax.dot_general(a, b, (((0,), (0,)), ((), ())), preferred_element_type=F32)


def cost(flops, nbytes, trans=0):
    return pl.CostEstimate(flops=int(flops), bytes_accessed=int(nbytes), transcendentals=int(trans))


def params(n_axes):
    sem = ("arbitrary",) * n_axes if n_axes else None
    return pltpu.CompilerParams(dimension_semantics=sem, vmem_limit_bytes=VMEM_LIMIT)


ANY = pl.BlockSpec(memory_space=pl.ANY)
SMEM = pl.BlockSpec(memory_space=pltpu.SMEM)


def all_of(a):
    return pl.BlockSpec(a.shape, lambda *_: (0,) * len(a.shape))


def corner(a):
    last = (min(a.shape[-2], 32 // a.dtype.itemsize), min(a.shape[-1], 128))
    return pl.BlockSpec((1,) * (a.ndim - 2) + last, lambda *_: (0,) * a.ndim)


def run(kernel, operands, specs, waits=(), prefetch=0, **kw):
    n, m = len(operands), len(waits)

    def body(*refs):
        return kernel(*refs[:n], *refs[n + m :])

    grid_spec = pltpu.PrefetchScalarGridSpec(
        num_scalar_prefetch=prefetch,
        grid=kw.pop("grid", (1,)),
        in_specs=[*specs, *[corner(a) for a in waits]],
        out_specs=kw.pop("out_specs"),
        scratch_shapes=kw.pop("scratch_shapes", ()),
    )
    return pl.pallas_call(body, grid_spec=grid_spec, **kw)(*operands, *waits)


class Blocks:
    def __init__(self, heads):
        self.heads = heads
        self.width = up128(heads * (HV + HQ))
        self.vals = heads * HV
        self.k0 = self.vals // 128 * 128
        self.kw = self.width - self.k0

    def stat(self, parts, i):
        return self.vals + i * 3 * (parts + 1)

    def window(self, i):
        wide = max(up128(j * HV % 128 + HV) for j in range(self.heads))
        first = i * HV
        return first, first // 128 * 128, wide


def lanes(shape, start=0):
    return lax.broadcasted_iota(jnp.int32, shape, len(shape) - 1) + start


def row(ref):
    return ref[...].reshape(1, -1)


def take(x, at, first):
    return jnp.sum(jnp.where((at >= first) & (at < first + 3), x, 0.0), axis=1, keepdims=True)


def three_terms(x):
    hi = x.astype(BF).astype(F32)
    mid = (x - hi).astype(BF).astype(F32)
    lo = (x - hi - mid).astype(BF).astype(F32)
    return hi, mid, lo


def norm_kernel(x_ref, g_ref, b_ref, r_ref, xh_ref, s_ref):
    step = min(256, x_ref.shape[1])

    @pl.loop(0, x_ref.shape[1] // step)
    def _(r):
        at = pl.ds(pl.multiple_of(r * step, step), step)
        x = x_ref[0, at, :].astype(F32)
        xc = x - jnp.mean(x, axis=1, keepdims=True)
        rstd = lax.rsqrt(jnp.mean(xc * xc, axis=1, keepdims=True) + EPS)
        xh = xc * rstd
        r_ref[0, at, :] = (xh * row(g_ref) + row(b_ref)).astype(BF)
        xh_ref[0, at, :] = xh.astype(BF)
        s_ref[0, at, :] = jnp.broadcast_to(rstd, (step, s_ref.shape[2]))


def byte_norm(x, g, b):
    seqs, slots, width = x.shape
    tile = min(1024, slots)
    at = lambda s, l: (s, l, 0)
    full = pl.BlockSpec((width,), lambda s, l: (0,))
    return pl.pallas_call(
        norm_kernel,
        grid=(seqs, slots // tile),
        in_specs=[pl.BlockSpec((1, tile, width), at), full, full],
        out_specs=[
            pl.BlockSpec((1, tile, width), at),
            pl.BlockSpec((1, tile, width), at),
            pl.BlockSpec((1, tile, 128), at),
        ],
        out_shape=[
            jax.ShapeDtypeStruct(x.shape, BF),
            jax.ShapeDtypeStruct(x.shape, BF),
            jax.ShapeDtypeStruct((seqs, slots, 128), F32),
        ],
        compiler_params=params(2),
        cost_estimate=cost(10 * x.size, 6 * x.size),
        name="byte_norm",
    )(x, g, b)


def own_latent_kernel(dp_ref, near_ref, far_ref, out_ref, cols):
    dp = dp_ref[0]
    halves = near_ref.shape[0]
    nl, d = out_ref.shape
    dl = d // (2 * halves)
    base = near_ref.shape[1] - dl
    for slot in range(2 * halves):
        src = (far_ref if slot % 2 else near_ref).at[slot // 2]
        cols[pl.ds(pl.multiple_of((dp ^ slot) * dl, 16), dl), :] = src[base:].astype(F32)
    out_ref[...] = cols[...].T[:nl].astype(BF)


def own_latents(nl, d, dp, near, far):
    vm = pl.BlockSpec(memory_space=pltpu.VMEM)
    return pl.pallas_call(
        own_latent_kernel,
        in_specs=[pl.BlockSpec(memory_space=pltpu.SMEM), vm, vm],
        out_specs=vm,
        out_shape=jax.ShapeDtypeStruct((nl, d), BF),
        scratch_shapes=[pltpu.VMEM((d, 128), F32)],
        compiler_params=params(0),
        cost_estimate=cost(nl * d, 8 * nl * d),
        name="own_latents",
    )(dp, near, far)


def latent_kernel(parts, *refs):
    ins, (g_ref, b_ref, out_ref) = refs[:parts], refs[parts:]
    nl = ins[0].shape[0]
    for k in range(parts):
        x = ins[k][...].astype(F32)
        xc = x - jnp.mean(x, axis=1, keepdims=True)
        xh = xc * lax.rsqrt(jnp.mean(xc * xc, axis=1, keepdims=True) + EPS)
        out_ref[k * nl : (k + 1) * nl] = (xh * row(g_ref) + row(b_ref)).astype(BF)


def latent_norm(lats, g, b):
    nl, d = lats[0].shape
    vm = pl.BlockSpec(memory_space=pltpu.VMEM)
    return pl.pallas_call(
        partial(latent_kernel, len(lats)),
        in_specs=[vm] * (len(lats) + 2),
        out_specs=vm,
        out_shape=jax.ShapeDtypeStruct((nl * len(lats), d), BF),
        compiler_params=params(0),
        cost_estimate=cost(10 * nl * len(lats) * d, 4 * nl * len(lats) * d),
        name="latent_norm",
    )(*lats, g, b)


def fwd_kernel(
    blk, parts, tiles, sc_ref, b_ref, near_ref, far_ref, lat_ref, kv_ref, p_ref, y_ref, w_ref, q_ref, wq, acc, cs, st
):
    s = pl.program_id(0)
    n = acc.shape[0]
    nl = n // parts
    slots, width = b_ref.shape[1:]
    d = lat_ref.shape[1]
    me = sc_ref[pl.num_programs(0)]

    @pl.when(s == 0)
    def _():
        dp = sc_ref[pl.num_programs(0) + 1]
        halves = near_ref.shape[0]
        cw, dl = width // (2 * halves), d // (2 * halves)
        for slot in range(2 * halves):
            src = (far_ref if slot % 2 else near_ref).at[slot // 2]
            at = dp ^ slot
            for t in range(tiles):
                w_ref[pl.ds(pl.multiple_of(at * cw, 16), cw), t * 128 : (t + 1) * 128] = src[
                    t * cw : (t + 1) * cw
                ]
            wq[pl.ds(pl.multiple_of(at * dl, 16), dl), :] = src[tiles * cw : tiles * cw + dl]
        q = nn(lat_ref[...], wq[...]).astype(BF).astype(F32)
        at = lanes(q.shape, blk.k0)
        for i in range(blk.heads):
            key = blk.vals + i * HQ
            q_ref[i * n : (i + 1) * n] = jnp.where((at >= key) & (at < key + HQ), q, 0.0).astype(BF)

    kv_ref[0] = nn(b_ref[0], w_ref[...]).astype(BF)

    mask = lanes((n, slots)) < sc_ref[s]
    acc[...] = jnp.zeros_like(acc)
    st[...] = jnp.zeros_like(st)

    for i in range(blk.heads):
        first, start, wide = blk.window(i)
        rows = pl.ds(i * n, n)
        sc = nt(q_ref[rows, :], kv_ref[0, :, blk.k0 :])
        sc = jnp.where(mask, sc, NEGATIVE)
        top = jnp.max(sc, axis=1, keepdims=True)
        p = jnp.exp2((sc - top) * SCALE2)
        total = jnp.sum(p, axis=1, keepdims=True)
        p = (p * (1.0 / total)).astype(BF)
        p_ref[0, rows, :] = p
        o = nn(p, kv_ref[0, :, pl.ds(start, wide)])
        at = lanes((n, wide)) + start
        acc[:, pl.ds(start, wide)] += jnp.where((at >= first) & (at < first + HV), o, 0.0)
        lse = top * SCALE2 + jnp.log(total) * LOG2E
        at = lanes(st.shape, blk.k0)
        for j, term in enumerate(three_terms(lse)):
            st[...] = jnp.where(at == blk.vals + 3 * i + j, term, st[...])

    y = acc[...]
    center = jnp.mean(y, axis=0, keepdims=True).astype(BF).astype(F32)
    y = y - center
    low = (y[:, blk.k0 :] + st[...]).astype(BF)
    y = y.astype(BF)
    for k in range(parts):
        to = pl.ds(pl.multiple_of(s * nl, nl), nl)
        if blk.k0:
            y_ref[me ^ k, to, : blk.k0] = y[k * nl : (k + 1) * nl, : blk.k0]
        y_ref[me ^ k, to, blk.k0 :] = low[k * nl : (k + 1) * nl]
    cs[...] = jnp.where(lax.broadcasted_iota(jnp.int32, cs.shape, 0) == s, center, cs[...])

    @pl.when(s == pl.num_programs(0) - 1)
    def _():
        rows = lax.broadcasted_iota(jnp.int32, cs.shape, 0)
        c = jnp.where(rows < pl.num_programs(0), cs[...], 0.0).astype(BF)
        for k in range(parts):
            y_ref[k, y_ref.shape[1] - 16 :, :] = c


def attend(blk, parts, scalars, bytes_r, near, far, lat_r, waits):
    seqs, slots, width = bytes_r.shape
    n, d = lat_r.shape
    tiles = blk.width // 128
    rows = seqs * (n // parts) + 16
    seq = lambda s, sc: (s, 0, 0)
    flat = lambda s, sc: (0, 0)
    whole = lambda s, sc: (0, 0, 0)
    flops = 2 * seqs * slots * (width * blk.width + blk.heads * n * (blk.kw + 256))
    return run(
        partial(fwd_kernel, blk, parts, tiles),
        (scalars, bytes_r, near, far, lat_r),
        [
            pl.BlockSpec((1, slots, width), seq),
            pl.BlockSpec(near.shape, whole),
            pl.BlockSpec(far.shape, whole),
            pl.BlockSpec(lat_r.shape, flat),
        ],
        waits,
        prefetch=1,
        grid=(seqs,),
        out_specs=[
            pl.BlockSpec((1, slots, blk.width), seq),
            pl.BlockSpec((1, blk.heads * n, slots), seq),
            pl.BlockSpec((parts, rows, blk.width), whole),
            pl.BlockSpec((width, blk.width), flat),
            pl.BlockSpec((blk.heads * n, blk.kw), flat),
            pl.BlockSpec((d, 128), flat),
        ],
        scratch_shapes=[
            pltpu.VMEM((n, blk.width), F32),
            pltpu.VMEM((16, blk.width), F32),
            pltpu.VMEM((n, blk.kw), F32),
        ],
        out_shape=[
            jax.ShapeDtypeStruct((seqs, slots, blk.width), BF),
            jax.ShapeDtypeStruct((seqs, blk.heads * n, slots), BF),
            jax.ShapeDtypeStruct((parts, rows, blk.width), BF),
            jax.ShapeDtypeStruct((width, blk.width), BF),
            jax.ShapeDtypeStruct((blk.heads * n, blk.kw), BF),
            jax.ShapeDtypeStruct((d, 128), BF),
        ],
        compiler_params=params(1),
        cost_estimate=cost(flops, 4 * seqs * slots * width, seqs * blk.heads * n * slots),
        name="attend_forward",
    )


def rows_kernel(blk, parts, seqs, order, *refs):
    me_ref, *refs = refs
    pays, refs = refs[:parts], refs[parts:]
    lat_ref, cot_ref, g_ref, b_ref, bh_ref, bb_ref, w_hbm = refs[:7]
    outs, refs = refs[7 : 7 + len(order)], refs[7 + len(order) :]
    out_ref, lx_ref, rx_ref, lm_ref, rm_ref, vec_ref, dsum_ref = refs[:7]
    w_ref, mix, st, mid_s, acc, pay_ref, dbh, sums, total_s, sems = refs[7:]
    me = me_ref[0]
    rows, d = acc.shape
    nl = rows // seqs
    ff = w_hbm.shape[2]
    fw = blk.vals
    back0 = fw // 128 * 128
    shift = fw - back0
    back = slice(back0, back0 + blk.width)
    out0 = up128(2 * fw)
    wide = slice(0, blk.width)
    low = slice(out0, out0 + blk.width)

    def copies():
        for t in range(parts):
            yield pltpu.make_async_copy(w_hbm.at[t], w_ref.at[t], sems.at[0])

    for c in copies():
        c.start()
    @pl.loop(0, seqs)
    def _(s):
        sl = pl.ds(pl.multiple_of(s * nl, nl), nl)
        for j in range(parts):
            ys = [pays[k ^ j][me ^ k, sl, :].astype(F32) for k in range(parts)]
            at = lanes((nl, blk.kw), blk.k0)
            stat = jnp.zeros((nl, blk.kw), F32)
            weights = []
            for i in range(blk.heads):
                lse = [take(y[:, blk.k0 :], at, blk.vals + 3 * i) for y in ys]
                top = lse[0]
                for x in lse[1:]:
                    top = jnp.maximum(top, x)
                es = [jnp.exp2(x - top) for x in lse]
                total = sum(es[1:], es[0])
                weights.append([e / total for e in es])
                for k in range(parts):
                    for q, term in enumerate(three_terms(weights[i][k])):
                        stat = jnp.where(at == blk.stat(parts, i) + 3 * k + q, term, stat)
            st[j, sl, :] = stat
            at = lanes((nl, blk.width))
            pick = (lax.broadcasted_iota(jnp.int32, (nl, 16), 1) == s).astype(BF)
            m = jnp.zeros((nl, blk.width), F32)
            for k in range(parts):
                wt = jnp.zeros((nl, blk.width), F32)
                for i in range(blk.heads):
                    wt = jnp.where((at >= i * HV) & (at < (i + 1) * HV), weights[i][k], wt)
                m = m + (ys[k] + nn(pick, pays[k ^ j][me ^ k, seqs * nl :, :])) * wt
            m = jnp.where(at < blk.vals, m, 0.0)
            mix[j, sl, :] = m
            rm_ref[j, sl, :] = m.astype(BF)

    for c in copies():
        c.wait()

    acc[...] = jnp.zeros_like(acc)

    @pl.loop(0, parts)
    def _(j):
        acc[...] += nt(rm_ref[j], w_ref[me ^ j, :, low])

    def centred(x):
        xc = x - jnp.mean(x, axis=1, keepdims=True)
        rstd = lax.rsqrt(jnp.mean(xc * xc, axis=1, keepdims=True) + EPS)
        return xc * rstd, rstd

    @pl.loop(0, seqs)
    def _(s):
        sl = pl.ds(pl.multiple_of(s * nl, nl), nl)
        mid = acc[sl, :] + lat_ref[...].astype(F32)
        mid_s[sl, :] = mid
        lx_ref[0, sl, :] = (centred(mid)[0] * row(g_ref) + row(b_ref)).astype(BF)
        lx_ref[1, sl, :] = cot_ref[sl, :].astype(BF)
        out_ref[sl, :] = mid + row(bb_ref)
        acc[sl, :] = jnp.zeros((nl, d), F32)

    @pl.loop(0, parts)
    def _(j):
        t = me ^ j
        live = lanes((rows, blk.width)) < fw
        pre = nn(lx_ref[0], w_ref[t, :, wide]) + bh_ref[t]
        phi = 0.5 * (1.0 + lax.erf(pre * math.sqrt(0.5)))
        slope = phi + pre * (jnp.exp(-0.5 * pre * pre) * (1.0 / math.sqrt(2.0 * math.pi)))
        act = jnp.where(live, pre * phi, 0.0)
        rx_ref[1, j] = (pltpu.roll(act, shift, 1) if shift else act).astype(BF)
        dact = nn(lx_ref[1], w_ref[t, :, back])
        dact = pltpu.roll(dact, blk.width - shift, 1) if shift else dact
        dpre = jnp.where(live, dact * slope, 0.0).astype(BF)
        rx_ref[0, j] = dpre
        dbh[t] = jnp.sum(dpre.astype(F32), axis=0, keepdims=True)
        out_ref[...] += nt(rx_ref[1, j], w_ref[t, :, back])
        acc[...] += nt(rx_ref[0, j], w_ref[t, :, wide])

    off = blk.vals - blk.k0
    sums[...] = jnp.zeros_like(sums)
    total_s[...] = jnp.zeros_like(total_s)

    @pl.loop(0, seqs)
    def _(s):
        sl = pl.ds(pl.multiple_of(s * nl, nl), nl)
        xh, rstd = centred(mid_s[sl, :])
        dy, cot = acc[sl, :], cot_ref[sl, :]
        for i, v in enumerate((dy * xh, dy, cot)):
            sums[i : i + 1] += jnp.sum(v, axis=0, keepdims=True)
        e = dy * row(g_ref)
        dv = rstd * (
            e - jnp.mean(e, axis=1, keepdims=True) - xh * jnp.mean(e * xh, axis=1, keepdims=True)
        )
        dmid = cot + dv
        lm_ref[sl, :] = dmid.astype(BF)
        total_s[off : off + nl] += dmid

    dsum_ref[...] = total_s[...].T.astype(BF)
    cuts = d // 128
    for i in range(3):
        for c in range(cuts):
            vec_ref[i * cuts + c : i * cuts + c + 1] = sums[i : i + 1, c * 128 : (c + 1) * 128]
    vec_ref[3 * cuts :] = jnp.zeros((vec_ref.shape[0] - 3 * cuts, 128), F32)
    for t in range(parts):
        first, move = t * fw // 128, t * fw % 128
        v = jnp.concatenate([dbh[t], jnp.zeros((1, 128), F32)], axis=1)
        v = pltpu.roll(v, move, 1) if move else v
        for c in range(v.shape[1] // 128):
            if first + c < cuts:
                vec_ref[3 * cuts + first + c : 3 * cuts + first + c + 1] += v[:, c * 128 : (c + 1) * 128]

    @pl.loop(0, parts)
    def _(j):
        dm = nn(lm_ref[...], w_ref[me ^ j, :, low]).astype(BF)
        prod = dm.astype(F32) * mix[j]
        at = lanes(prod.shape)
        stat = st[j]
        at_k = lanes(stat.shape, blk.k0)
        for i in range(blk.heads):
            inner = jnp.sum(
                jnp.where((at >= i * HV) & (at < (i + 1) * HV), prod, 0.0), axis=1, keepdims=True
            )
            for q, term in enumerate(three_terms(inner)):
                stat = jnp.where(at_k == blk.stat(parts, i) + 3 * parts + q, term, stat)
        if blk.k0:
            pay_ref[j, :, : blk.k0] = dm[:, : blk.k0]
        pay_ref[j, :, blk.k0 :] = jnp.where(at_k < blk.vals, dm[:, blk.k0 :].astype(F32), stat).astype(BF)

    for out, stages in zip(outs, order, strict=True):
        for i, stage in enumerate(stages):
            for k in range(parts):
                out[me ^ k, i] = pay_ref[stage ^ k]


def rows_step(blk, parts, seqs, order, me, pays, lat, cot, g, b, bh, bb, w):
    rows, d = cot.shape
    nl = rows // seqs
    whole = lambda a: pl.BlockSpec(a.shape, lambda i, me, r=len(a.shape): (0,) * r)
    outs = [jax.ShapeDtypeStruct((parts, len(o), rows, blk.width), BF) for o in order] + [
        jax.ShapeDtypeStruct((rows, d), F32),
        jax.ShapeDtypeStruct((2, rows, d), BF),
        jax.ShapeDtypeStruct((2, parts, rows, blk.width), BF),
        jax.ShapeDtypeStruct((rows, d), BF),
        jax.ShapeDtypeStruct((parts, rows, blk.width), BF),
        jax.ShapeDtypeStruct(((4 * d // 128 + 7) // 8 * 8, 128), F32),
        jax.ShapeDtypeStruct((d, 128), BF),
    ]
    return pl.pallas_call(
        partial(rows_kernel, blk, parts, seqs, order),
        grid_spec=pltpu.PrefetchScalarGridSpec(
            num_scalar_prefetch=1,
            grid=(1,),
            in_specs=[whole(a) for a in pays]
            + [whole(a) for a in (lat, cot, g, b, bh, bb)]
            + [ANY],
            out_specs=[whole(o) for o in outs],
            scratch_shapes=[
                pltpu.VMEM((parts, d, w.shape[-1]), BF),
                pltpu.VMEM((parts, rows, blk.width), F32),
                pltpu.VMEM((parts, rows, blk.kw), F32),
                pltpu.VMEM((rows, d), F32),
                pltpu.VMEM((rows, d), F32),
                pltpu.VMEM((parts, rows, blk.width), BF),
                pltpu.VMEM((parts, 1, blk.width), F32),
                pltpu.VMEM((8, d), F32),
                pltpu.VMEM((128, d), F32),
                pltpu.SemaphoreType.DMA((1,)),
            ],
        ),
        out_shape=outs,
        compiler_params=params(1),
        cost_estimate=cost(12 * rows * d * d, 2 * w.size + 40 * rows * d, 2 * rows * d),
        name="rows",
    )(me, *pays, lat, cot, g, b, bh, bb, w)


def ff_kernel(blk, me_ref, lh_ref, lo_ref, rd_ref, ra_ref, out_ref):
    fw = blk.vals
    back0 = fw // 128 * 128
    hid = tn(lh_ref[0], rd_ref[0, 0])
    back = tn(lo_ref[0], ra_ref[0, 0])
    dps, _, dl, wide = out_ref.shape
    cuts = [(0, back0, hid[:, :back0])] if back0 else []
    if back0 < blk.width:
        n = blk.width - back0
        cuts.append((back0, n, hid[:, back0:] + back[:, :n]))
        cuts.append((blk.width, wide - blk.width, back[:, n : n + wide - blk.width]))
    for at, n, piece in cuts:
        if n:
            out_ref[:, 0, :, at : at + n] = piece.astype(BF).reshape(dps, dl, n)


def ff_grads(blk, me, dps, lx, rx):
    _, parts, rows, width = rx.shape
    d = lx.shape[2]
    wide = up128(2 * blk.vals)
    return pl.pallas_call(
        partial(ff_kernel, blk),
        grid_spec=pltpu.PrefetchScalarGridSpec(
            num_scalar_prefetch=1,
            grid=(parts,),
            in_specs=[
                pl.BlockSpec((1, rows, d), lambda i, me: (0, 0, 0)),
                pl.BlockSpec((1, rows, d), lambda i, me: (1, 0, 0)),
                pl.BlockSpec((1, 1, rows, width), lambda i, me: (0, i, 0, 0)),
                pl.BlockSpec((1, 1, rows, width), lambda i, me: (1, i, 0, 0)),
            ],
            out_specs=pl.BlockSpec((dps, 1, d // dps, wide), lambda i, me: (0, me[0] ^ i, 0, 0)),
        ),
        out_shape=jax.ShapeDtypeStruct((dps, parts, d // dps, wide), BF),
        compiler_params=params(1),
        cost_estimate=cost(4 * parts * rows * d * width, 4 * parts * d * width),
        name="ff_grads",
    )(me, lx, lx, rx, rx)


def slot_place(slot, dps):
    return (slot & 1) * (dps // 2) + (slot >> 1)


def core_slot(core, i, half):
    return core * half + ((i ^ (1 - core)) if half > 1 else i)


def out_kernel(half, dps, sc_ref, lx_ref, rx_ref, lx2_ref, rx2_ref, *outs):
    core, dp = sc_ref[0], sc_ref[1]
    dl = lx_ref.shape[1] // dps
    for i, out_ref in enumerate(outs):
        slot = core_slot(core, i, half)
        r = (tn(lx_ref[...], rx_ref[slot]) + tn(lx2_ref[...], rx2_ref[slot])).astype(BF)
        for z in range(dps):
            out_ref[slot_place(dp ^ z, dps)] = r[z * dl : (z + 1) * dl]


def out_grads(scalars, dps, lx, rx, lx2, rx2, waits):
    parts, rows, width = rx.shape
    d = lx.shape[1]
    half = max(parts // 2, 1)
    whole = lambda a: pl.BlockSpec(a.shape, lambda i, sc, r=len(a.shape): (0,) * r)
    outs = [jax.ShapeDtypeStruct((dps, d // dps, width), BF)] * half
    return run(
        partial(out_kernel, half, dps),
        (scalars, lx, rx, lx2, rx2),
        [whole(a) for a in (lx, rx, lx2, rx2)],
        waits,
        prefetch=1,
        out_specs=[whole(o) for o in outs],
        out_shape=outs,
        compiler_params=params(1),
        cost_estimate=cost(4 * half * rows * d * width, 2 * half * d * width),
        name="out_grads",
    )


def bwd_kernel(blk, parts, dps, ks, add, before, sc_ref, *refs):
    count = len(ks)
    kvs, ps, qs, ws, refs = (
        refs[:count],
        refs[count : 2 * count],
        refs[2 * count : 3 * count],
        refs[3 * count : 4 * count],
        refs[4 * count :],
    )
    xh_ref, g_ref, b_ref, dm_ref, *refs = refs
    extra, refs = refs[:add], refs[add:]
    earlier, refs = (refs[: 2 * before + 1], refs[2 * before + 1 :]) if add else ((), refs)
    dkvs, gws, refs = refs[:count], refs[count : 2 * count], refs[2 * count :]
    *sums, dkvt, gacc, sacc, dmx, dqs, dqg = refs
    me, dp = sc_ref[0], sc_ref[1]
    s = pl.program_id(0)
    n = dmx.shape[1]
    nl = n // parts
    off, qk = blk.vals - blk.k0, blk.heads * HQ

    @pl.when(s == 0)
    def _():
        gacc[...] = jnp.zeros_like(gacc)
        sacc[...] = jnp.zeros_like(sacc)
        dqs[...] = jnp.zeros_like(dqs)

    for c in range(count):
        kv_ref, p_ref = kvs[c], ps[c]
        for k in range(parts):
            dmx[c, k * nl : (k + 1) * nl] = dm_ref[me ^ k, c]
        tail = dmx[c, :, blk.k0 :].astype(F32)
        at_k = lanes(tail.shape, blk.k0)
        at_n = lax.broadcasted_iota(jnp.int32, (n, 1), 0)
        dkvt[c] = jnp.zeros_like(dkvt[c])
        for i in range(blk.heads):
            first, start, width = blk.window(i)
            rows = pl.ds(i * n, n)
            cols = pl.ds(start, width)
            stat = blk.stat(parts, i)
            ratio = take(tail, at_k, stat)
            for k in range(1, parts):
                ratio = jnp.where(at_n >= k * nl, take(tail, at_k, stat + 3 * k), ratio)
            inner = take(tail, at_k, stat + 3 * parts)
            at = lanes((n, width)) + start
            dm = dmx[c, :, cols].astype(F32)
            dm = jnp.where((at >= first) & (at < first + HV), dm, 0.0)
            dpr = nt(dm.astype(BF), kv_ref[0, :, cols])
            ds = (p_ref[0, rows, :].astype(F32) * ((dpr - inner) * (ratio * SCALE))).astype(BF)
            dkvt[c, cols, :] += tn((dm * ratio).astype(BF), p_ref[0, rows, :])
            dkvt[c, blk.k0 :, :] += tn(qs[c][rows, :], ds)
            dq = nn(ds, kv_ref[0, :, blk.k0 :])
            key = blk.vals + i * HQ
            dqs[c] += jnp.where((at_k >= key) & (at_k < key + HQ), dq, 0.0)

        low = dkvt[c].astype(BF)
        dkvs[c][0] = low.T
        gacc[c] += nn(low, xh_ref[0])
        sacc[c] += jnp.sum(low.astype(F32), axis=1, keepdims=True)

    @pl.when(s == pl.num_programs(0) - 1)
    def _():
        dg, db = 0.0, 0.0
        for c in range(count):
            wt = ws[c][...].T.astype(F32)
            grad, col = gacc[c], sacc[c, :, 0:1]
            dg = dg + jnp.sum(wt * grad, axis=0, keepdims=True)
            db = db + jnp.sum(wt * col, axis=0, keepdims=True)
            gw = (grad * row(g_ref) + col * row(b_ref)).T.astype(BF)
            cl = gw.shape[0] // dps
            for z in range(dps):
                gws[c][slot_place(dp ^ z, dps), :cl] = gw[z * cl : (z + 1) * cl]
            if add and c == count - 1:
                more = jnp.where(dp % 2 == 0, extra[0][...].astype(F32), 0.0)
                for e in extra[1:-1]:
                    more = more + e[...].astype(F32)
                gws[c][:, cl:] = more.astype(BF)
                dl = extra[-1].shape[0] // dps
                for z in range(dps):
                    to = slot_place(dp ^ z, dps)
                    beside = gws[c][to, cl:, blk.k0 :].astype(F32) + extra[-1][z * dl : (z + 1) * dl].astype(F32)
                    gws[c][to, cl:, blk.k0 :] = beside.astype(BF)
            for k in range(parts):
                dqg[pl.ds(pl.multiple_of((me ^ k) * nl, 8), nl), :] = dqs[c, k * nl : (k + 1) * nl]
            left = pltpu.roll(dqg[: n // 2], (128 - off) % 128, 1)
            right = pltpu.roll(dqg[n // 2 :], (64 - off) % 128, 1)
            dqs[c, : n // 2] = left + right
        head = parts * (n // 2)
        if add:
            (msg,) = sums
            gains = earlier[2 * before].shape[0]
            first = msg.shape[0] - gains
            msg[:head] = sum((r[...] for r in earlier[1:before]), earlier[0][...]) if before else jnp.zeros((head, 128), F32)
            msg[head:first] = (
                sum((r[...] for r in earlier[before + 1 : 2 * before]), earlier[before][...])
                if before
                else jnp.zeros((first - head, 128), F32)
            )
            msg[first:] = earlier[2 * before][...]
            at, gain = msg, head
        else:
            at, small = sums
            at[...] = jnp.zeros_like(at)
            small[...] = jnp.zeros_like(small)
        for c, k in enumerate(ks):
            at[pl.ds(pl.multiple_of((me ^ k) * (n // 2), 8), n // 2), :] += dqs[c, : n // 2]
        if add:
            small, base = msg, gain
        else:
            base = 0
        cuts = dg.shape[1] // 128
        for i, v in enumerate((dg, db)):
            for c in range(cuts):
                r = base + i * cuts + c
                small[r : r + 1] += v[:, c * 128 : (c + 1) * 128]


def attend_backward(blk, parts, dps, ks, scalars, kvs, ps, qs, ws, xh, g, b, pay, extra, earlier, waits):
    seqs, slots, width = xh.shape
    count = len(kvs)
    n = qs[0].shape[0] // blk.heads
    nl = n // parts
    seq = lambda s, sc: (s, 0, 0)
    cl = width // dps
    sizes = [cl] * count
    if extra:
        sizes[-1] += extra[0].shape[1]
    outs = (
        [jax.ShapeDtypeStruct((seqs, slots, blk.width), BF)] * count
        + [jax.ShapeDtypeStruct((dps, r, blk.width), BF) for r in sizes]
    )
    head, gains = parts * (n // 2), (2 * width // 128 + 7) // 8 * 8
    if extra:
        outs = outs + [jax.ShapeDtypeStruct((head + gains + earlier[-1].shape[0], 128), F32)]
    else:
        outs = outs + [jax.ShapeDtypeStruct((head, 128), F32), jax.ShapeDtypeStruct((gains, 128), F32)]
    res = run(
        partial(bwd_kernel, blk, parts, dps, tuple(ks), len(extra), len(earlier) // 2),
        (scalars, *kvs, *ps, *qs, *ws, xh, g, b, pay, *extra, *earlier),
        [pl.BlockSpec((1, slots, blk.width), seq)] * count
        + [pl.BlockSpec((1, blk.heads * n, slots), seq)] * count
        + [all_of(a) for a in (*qs, *ws)]
        + [
            pl.BlockSpec((1, slots, width), seq),
            all_of(g),
            all_of(b),
            pl.BlockSpec((parts, count, nl, blk.width), lambda s, sc: (0, 0, s, 0)),
        ]
        + [all_of(a) for a in (*extra, *earlier)],
        waits,
        prefetch=1,
        grid=(seqs,),
        out_specs=[pl.BlockSpec((1, slots, blk.width), seq)] * count + [all_of(o) for o in outs[count:]],
        scratch_shapes=[
            pltpu.VMEM((count, blk.width, slots), F32),
            pltpu.VMEM((count, blk.width, width), F32),
            pltpu.VMEM((count, blk.width, 128), F32),
            pltpu.VMEM((count, n, blk.width), BF),
            pltpu.VMEM((count, n, blk.kw), F32),
            pltpu.VMEM((n, blk.kw), F32),
        ],
        out_shape=outs,
        compiler_params=params(1),
        cost_estimate=cost(
            2 * count * seqs * slots * (width * blk.width + 4 * blk.heads * n * 256),
            (2 + 4 * count) * seqs * slots * width,
        ),
        name="attend_backward",
    )
    return res[:count], res[count : 2 * count], res[2 * count :]


def bytes_kernel(parts, *refs):
    dkvs, ws = refs[:parts], refs[parts : 2 * parts]
    xh_ref, s_ref, g_ref, *_, out_ref, done_ref = refs[2 * parts :]
    done_ref[...] = jnp.zeros_like(done_ref)
    step = min(256, out_ref.shape[1])

    @pl.loop(0, out_ref.shape[1] // step)
    def _(r):
        at = pl.ds(pl.multiple_of(r * step, step), step)
        dy = nt(dkvs[0][0, at, :], ws[0][...])
        for k in range(1, parts):
            dy = dy + nt(dkvs[k][0, at, :], ws[k][...])
        xh = xh_ref[0, at, :].astype(F32)
        e = dy * row(g_ref)
        me = jnp.mean(e, axis=1, keepdims=True)
        mx = jnp.mean(e * xh, axis=1, keepdims=True)
        out_ref[0, at, :] = s_ref[0, at, 0:1] * (e - me - xh * mx)


def byte_grads(first, count, dkvs, ws, xh, rstd, g, into, waits):
    _, slots, width = xh.shape
    bw = ws[0].shape[1]
    tile = min(512, slots)
    at = lambda s, l: (first + s, l, 0)
    flat = lambda s, l: (0, 0)
    kept = [] if into is None else [into]
    return run(
        partial(bytes_kernel, len(ws)),
        (*dkvs, *ws, xh, rstd, g, *kept),
        [pl.BlockSpec((1, tile, bw), at) for _ in dkvs]
        + [pl.BlockSpec((width, bw), flat) for _ in ws]
        + [
            pl.BlockSpec((1, tile, width), at),
            pl.BlockSpec((1, tile, 128), at),
            all_of(g),
        ]
        + [ANY] * len(kept),
        waits,
        grid=(count, slots // tile),
        out_specs=[pl.BlockSpec((1, tile, width), at), pl.BlockSpec((8, 128), flat)],
        out_shape=[jax.ShapeDtypeStruct(xh.shape, F32), jax.ShapeDtypeStruct((8, 128), BF)],
        input_output_aliases={2 * len(ws) + 3: 0} if kept else {},
        compiler_params=params(2),
        cost_estimate=cost(2 * count * slots * width * bw * len(ws), 10 * count * slots * width),
        name="byte_grads",
    )


def merge_kernel(cl, own_ref, *refs):
    more, (keep_ref, send_ref) = refs[:-2], refs[-2:]
    h = keep_ref.shape[0]
    for i in range(2 * h):
        out, at = (keep_ref, i) if i < h else (send_ref, i - h)
        x = own_ref[i, :cl].astype(F32)
        for r in more:
            x = x + r[i].astype(F32)
        out[at, :cl] = x.astype(BF)
        out[at, cl:] = own_ref[i, cl:]


def merge(own, more, waits):
    dps, rows, bw = own.shape
    cl = more[0].shape[1]
    out = jax.ShapeDtypeStruct((dps // 2, rows, bw), BF)
    return run(
        partial(merge_kernel, cl),
        (own, *more),
        [all_of(a) for a in (own, *more)],
        waits,
        out_specs=[all_of(out)] * 2,
        out_shape=[out] * 2,
        compiler_params=params(1),
        cost_estimate=cost(own.size * len(more), own.size * 6),
        name="merge",
    )


def plus_kernel(a_ref, b_ref, out_ref):
    out_ref[...] = a_ref[...] + b_ref[...]


def plus(a, b, waits):
    return run(
        plus_kernel,
        (a, b),
        [all_of(a)] * 2,
        waits,
        out_specs=all_of(a),
        out_shape=jax.ShapeDtypeStruct(a.shape, a.dtype),
        compiler_params=params(1),
        cost_estimate=cost(a.size, 12 * a.size),
        name="plus",
    )


def split_kernel(keep_ref, got_ref, own_ref, *outs):
    own_ref[...] = keep_ref[0].astype(F32) + got_ref[0].astype(F32)
    for z, out in enumerate(outs):
        out[...] = (keep_ref[z + 1].astype(F32) + got_ref[z + 1].astype(F32)).astype(BF)


def split(keep, got):
    h, rows, bw = keep.shape
    vm = pl.BlockSpec(memory_space=pltpu.VMEM)
    return pl.pallas_call(
        split_kernel,
        in_specs=[vm, vm],
        out_specs=[vm] * h,
        out_shape=[jax.ShapeDtypeStruct((rows, bw), F32)] + [jax.ShapeDtypeStruct((rows, bw), BF)] * (h - 1),
        compiler_params=params(0),
        cost_estimate=cost(keep.size, keep.size * 6),
        name="split",
    )(keep, got)


def final_kernel(blk, parts, dps, near, sc_ref, *refs):
    own_ref, refs = refs[0], refs[1:]
    gots, refs = refs[:near], refs[near:]
    ff_ref, msg_ref, refs = refs[0], refs[1], refs[2:]
    lat_refs, lqs, refs = refs[:parts], refs[parts : 2 * parts], refs[2 * parts :]
    g_ref, b_ref, gv_ref, gk_ref, go_ref, gh_ref, gb_ref, gq_ref, gl_ref, sg_ref, sb_ref, *vecs = refs[:-3]
    dys, tr, dqx = refs[-3:]
    me, dp = sc_ref[0], sc_ref[1]
    nl, d = lat_refs[0].shape
    n = nl * parts
    h = n // 2
    dl = d // dps
    off, qk, fw = blk.vals - blk.k0, blk.heads * HQ, blk.vals
    total = own_ref[...]
    for r in gots:
        total = total + r[...].astype(F32)
    cl = gv_ref.shape[0]
    gv_ref[...] = total[:cl, : blk.vals]
    gk_ref[...] = total[:cl, blk.k0 :].T[off : off + qk]
    go_ref[...] = total[cl:, :fw]
    rows_sum = total[cl:, blk.k0 :].T[off : off + nl]
    both = ff_ref[0].astype(F32)
    for k in range(1, parts):
        both = both + ff_ref[k].astype(F32)
    gh_ref[...] = both[:, :fw]
    back0 = fw // 128 * 128
    tail = both[:, back0:]
    shift = fw - back0
    tail = pltpu.roll(tail, tail.shape[1] - shift, 1) if shift else tail
    gb_ref[...] = tail[:, :fw]
    at = lanes((h, 128))
    dys[...] = jnp.zeros_like(dys)
    for k in reversed(range(parts)):
        block = msg_ref[pl.ds(pl.multiple_of((me ^ k) * h, 8), h), :]
        dqx[:h] = pltpu.roll(jnp.where(at < 64, block, 0.0), off, 1)
        dqx[h:] = pltpu.roll(jnp.where(at >= 64, block, 0.0), (off + 64) % 128, 1)
        dys[...] += nt(dqx[...].astype(BF), lqs[k][...])
    g, b = row(g_ref), row(b_ref)
    dg, db = jnp.zeros((1, d), F32), jnp.zeros((1, d), F32)
    for k in range(parts):
        rows = pl.ds(pl.multiple_of((me ^ k) * nl, 8), nl)
        x = lat_refs[k][...].astype(F32)
        xc = x - jnp.mean(x, axis=1, keepdims=True)
        rs = lax.rsqrt(jnp.mean(xc * xc, axis=1, keepdims=True) + EPS)
        xh = xc * rs
        dy = dys[rows, :]
        dg = dg + jnp.sum(dy * xh, axis=0, keepdims=True)
        db = db + jnp.sum(dy, axis=0, keepdims=True)
        if k == 0:
            e = dy * g
            keep = rs * (
                e - jnp.mean(e, axis=1, keepdims=True) - xh * jnp.mean(e * xh, axis=1, keepdims=True)
            )
        dys[rows, :] = xh * g + b
    sg_ref[...] = dg[0]
    sb_ref[...] = db[0]
    tr[...] = dys[...].T
    here = pl.ds(pl.multiple_of(dp * dl, 8), dl)
    mine = tr[here, :].astype(BF)
    gq = lax.dot_general(dqx[...].astype(BF), mine, (((0,), (1,)), ((), ())), preferred_element_type=F32)
    gq_ref[...] = gq[off : off + qk]
    tr[:, :nl] = keep.T
    gl_ref[...] = tr[here, :nl].T + rows_sum
    first = parts * h
    gains = (2 * vecs[0].shape[0] // 128 + 7) // 8 * 8
    start = first
    for i, ref in enumerate(vecs):
        if i == 2:
            start = first + gains
        for c in range(ref.shape[0] // 128):
            ref[c * 128 : (c + 1) * 128] = msg_ref[start + c : start + c + 1].reshape(128)
        start += ref.shape[0] // 128


def final(blk, dps, scalars, own, gots, ff, msg, lats, lqs, g, b, width, cl):
    parts = len(lats)
    nl, d = lats[0].shape
    n = nl * parts
    dl = d // dps
    qk, fw = blk.heads * HQ, blk.vals
    vm = pl.BlockSpec(memory_space=pltpu.VMEM)
    shapes = [(cl, blk.vals), (qk, cl), (dl, fw), (dl, fw), (dl, fw), (qk, dl), (nl, dl), (d,), (d,)]
    shapes += [(width,), (width,), (d,), (d,), (d,), (d,)]
    return pl.pallas_call(
        partial(final_kernel, blk, parts, dps, len(gots)),
        in_specs=[SMEM] + [vm] * (5 + len(gots) + 2 * parts),
        out_specs=[vm] * len(shapes),
        out_shape=[jax.ShapeDtypeStruct(s, F32) for s in shapes],
        scratch_shapes=[pltpu.VMEM((n, d), F32), pltpu.VMEM((d, n), F32), pltpu.VMEM((n, 128), F32)],
        compiler_params=params(0),
        cost_estimate=cost(2 * n * 128 * d * parts, 12 * d * n),
        name="final",
    )(scalars, own, *gots, ff, msg, *lats, *lqs, g, b)


def on_device(
    dps,
    parts,
    byte_in,
    lengths,
    latent,
    g_in,
    b_in,
    g_lat,
    b_lat,
    w_query,
    w_key,
    w_value,
    w_out,
    g_mlp,
    b_mlp,
    w_hidden,
    b_hidden,
    w_back,
    b_back,
    cotangent,
):
    seqs, slots, width = byte_in.shape
    nl, dl = latent.shape
    n, d = nl * parts, dl * dps
    blk = Blocks(w_key.shape[1] // HQ)
    qk = w_key.shape[1]
    bw = blk.width
    me = lax.axis_index("tensor").astype(jnp.int32)
    dp = lax.axis_index("dp").astype(jnp.int32)
    core = dp % 2

    def hop(x, k):
        return lax.ppermute(x, "tensor", [(i, i ^ k) for i in range(parts)])

    def hop_dp(x, k):
        return lax.ppermute(x, "dp", [(i, i ^ k) for i in range(dps)])

    def swap(x):
        return lax.all_to_all(x, "tensor", split_axis=0, concat_axis=0, tiled=True)

    def widen(x):
        return jnp.pad(x, ((0, 0), (0, bw - x.shape[1])))

    def after(x, *others):
        return lax.optimization_barrier((x, *others))[0]

    fw = d // parts
    mats = jnp.concatenate([w_hidden, w_back.T], axis=1)
    mats = jnp.pad(mats, ((0, 0), (0, up128(2 * fw) - 2 * fw)))
    mats = jnp.concatenate([mats, widen(w_out.T)], axis=1)

    tiles = bw // 128
    off = blk.vals - blk.k0
    dp1, me1 = dp.reshape(1), me.reshape(1)
    shard = widen(jnp.concatenate([w_value, w_key], axis=1))
    lq = jnp.concatenate([jnp.pad(latent.T, ((0, 0), (0, off - nl))), w_query], axis=1)
    lq = jnp.pad(lq, ((0, 0), (0, 128 - off - qk)))
    shard = jnp.concatenate([shard[:, t * 128 : (t + 1) * 128] for t in range(tiles)] + [lq], axis=0)
    got = [hop_dp(shard, j) for j in range(2, dps, 2)]
    bytes_r, xh, rstd = byte_norm(after(byte_in, shard), g_in, b_in)
    near = after(jnp.stack([shard] + got, axis=0), rstd)
    far = hop_dp(near, 1)
    lat = own_latents(nl, d, dp1, near, far)
    lats = [lat] + [hop(lat, k) for k in range(1, parts)]
    lat_r = latent_norm(lats, g_lat, b_lat)
    gate = lax.optimization_barrier((near, far, *lats))
    nears = [near] + [hop(gate[0], k) for k in range(1, parts)]
    fars = [far]
    mats = lax.all_gather(after(mats, gate[0]), ("tensor", "dp"), axis=0, tiled=True).reshape(parts, d, -1)

    live = jnp.clip(lengths - me * slots, 0, slots).astype(jnp.int32)
    scalars = jnp.concatenate([live, me1, dp1])
    kvs, ps, ws, qs, lqs, pays = [], [], [], [], [], []
    for k in range(parts):
        waits = []
        if k == 1:
            late = lax.optimization_barrier((kvs[0], *nears[1:]))[1:]
            fars += [hop_dp(a, 1) for a in late]
        if k:
            waits.append(kvs[k - 1])
        if k > 1:
            waits.append(pays[k - 2])
        kv, p, y, w, q, lq = attend(blk, parts, scalars, bytes_r, nears[k], fars[k], lat_r, waits)
        kvs.append(kv)
        ps.append(p)
        ws.append(w)
        qs.append(q)
        lqs.append(lq)
        pays.append(swap(y))

    rows = seqs * nl
    bh = jnp.pad(b_hidden.reshape(parts, 1, -1), ((0, 0), (0, 0), (0, bw - fw)))
    slots_left = list(range(1, parts)) + [0]
    order = [slots_left[i : i + 2] for i in range(0, parts, 2)]
    res = rows_step(
        blk,
        parts,
        seqs,
        order,
        jnp.stack([me, core]),
        pays,
        lat,
        cotangent.reshape(rows, d),
        g_mlp,
        b_mlp,
        bh,
        b_back,
        mats,
    )
    dpays, (out, lx, rx, lm, rm, vec_rows, dsum) = res[: len(order)], res[len(order) :]
    latents_out = out.reshape(seqs, nl, d)
    dpays = [swap(a) for a in dpays]
    lm2, rm2 = hop_dp(lm, 1), hop_dp(rm, 1)
    ff = ff_grads(blk, me1, dps, lx, rx)
    scalars = jnp.stack([me, dp])
    pairs = out_grads(jnp.stack([core, dp]), dps, lm, rm, lm2, rm2, [ff])
    half = len(pairs)
    moved = []
    for i in range(half):
        perm = []
        for z in range(dps):
            for t in range(parts):
                c = z % 2
                slot = c * half + ((i ^ (1 - c)) if half > 1 else i)
                if slot:
                    perm.append((z * parts + t, z * parts + (t ^ slot)))
        moved.append(lax.ppermute(pairs[i], ("dp", "tensor"), perm))
    ff = lax.psum_scatter(ff, "dp", scatter_dimension=0, tiled=True).reshape(parts, dl, -1)

    dkvs, gws, dqs, dgbs = [None] * parts, [None] * parts, [], []
    for at, ks in enumerate(order):
        last = at == len(order) - 1
        got, grads, sums = attend_backward(
            blk,
            parts,
            dps,
            ks,
            scalars,
            [kvs[k] for k in ks],
            [ps[k] for k in ks],
            [qs[k] for k in ks],
            [ws[k] for k in ks],
            xh,
            g_in,
            b_in,
            dpays[at],
            [pairs[min(1, half - 1)], *moved, dsum] if last else [],
            [*dqs, *dgbs, vec_rows] if last else [],
            [pairs[0]] if at == 0 else [],
        )
        for i, k in enumerate(ks):
            dkvs[k] = got[i]
            gws[k] = hop(grads[i], k) if k else grads[i]
        if not last:
            dqs.append(sums[0])
            dgbs.append(sums[1])
    (msg,) = sums

    cl = width // dps
    h = dps // 2
    wide_steps = [(hop_dp, 2**i) for i in reversed(range(1, dps.bit_length() - 1))]
    steps = [(hop_dp, 1), wide_steps[0]] + [(hop, 2**i) for i in range(parts.bit_length() - 1)] + wide_steps[1:]
    grad_bytes = None
    group = max(seqs // 2, 1)
    todo = list(range(0, seqs, group))
    done = []

    def cover(*waits):
        nonlocal grad_bytes, done
        if todo:
            grad_bytes, token = byte_grads(todo.pop(0), group, dkvs, ws, xh, rstd, g_in, grad_bytes, waits)
            done = [token]

    def sent(msg):
        f, j = steps.pop(0)
        return f(msg, j)

    msg = msg + sent(msg)
    got = sent(msg)
    cover(msg, *[gws[k] for ks in order[:-1] for k in ks])
    keep, send = merge(gws[0], [gws[k] for ks in order for k in ks if k], [*done, got])
    far = hop_dp(send, 1)
    msg = plus(msg, got, done)
    other = sent(msg)
    own, *low = split(keep, far)
    got = [hop_dp(low[z - 1], 2 * z) for z in range(1, h)]
    ff = swap(ff)
    while todo:
        cover(msg, *low)
    msg = plus(msg, other, [*done, *got])
    while steps:
        msg = msg + sent(msg)

    gv, gk, go, gh, gb, gq, gl, sum_g_lat, sum_b_lat, sum_g_in, sum_b_in, sum_g_mlp, sum_b_mlp, sum_back, sum_hidden = final(
        blk, dps, scalars, own, got, ff, msg, lats, lqs, g_lat, b_lat, width, cl
    )
    return (
        latents_out,
        grad_bytes,
        gl,
        sum_g_in,
        sum_b_in,
        sum_g_lat,
        sum_b_lat,
        gq.T,
        gk.T,
        gv,
        go.T,
        sum_g_mlp,
        sum_b_mlp,
        gh,
        sum_hidden,
        gb.T,
        sum_back,
    )


def solution(mesh):
    return jax.shard_map(
        partial(on_device, mesh.shape["dp"], mesh.shape["tensor"]),
        mesh=mesh,
        in_specs=(
            P("dp", "tensor", None),
            P("dp"),
            P("tensor", "dp"),
            P(),
            P(),
            P(),
            P(),
            P("dp", "tensor"),
            P("dp", "tensor"),
            P("dp", "tensor"),
            P("tensor", "dp"),
            P(),
            P(),
            P("dp", "tensor"),
            P(),
            P("tensor", "dp"),
            P(),
            P("dp", "tensor", None),
        ),
        out_specs=(
            P("dp", "tensor", None),
            P("dp", "tensor", None),
            P("tensor", "dp"),
            P(),
            P(),
            P(),
            P(),
            P("dp", "tensor"),
            P("dp", "tensor"),
            P("dp", "tensor"),
            P("tensor", "dp"),
            P(),
            P(),
            P("dp", "tensor"),
            P(),
            P("tensor", "dp"),
            P(),
        ),
        check_vma=False,
    )
```

```python
from functools import partial
import math

import jax
import jax.numpy as jnp
from jax import lax
from jax.experimental import pallas as pl
from jax.experimental.pallas import tpu as pltpu
from jax.sharding import PartitionSpec as P

HQ = 32
HV = 160
EPS = 1e-05
NEGATIVE = -1e30
SCALE = HQ**-0.5
LOG2E = math.log2(math.e)
SCALE2 = SCALE * LOG2E
BF = jnp.bfloat16
F32 = jnp.float32
VMEM_LIMIT = 60 << 20


def up128(n):
    return (n + 127) // 128 * 128


def nn(a, b):
    return lax.dot_general(a, b, (((1,), (0,)), ((), ())), preferred_element_type=F32)


def nt(a, b):
    return lax.dot_general(a, b, (((1,), (1,)), ((), ())), preferred_element_type=F32)


def tn(a, b):
    return lax.dot_general(a, b, (((0,), (0,)), ((), ())), preferred_element_type=F32)


def cost(flops, nbytes, trans=0):
    return pl.CostEstimate(flops=int(flops), bytes_accessed=int(nbytes), transcendentals=int(trans))


def params(n_axes):
    sem = ("arbitrary",) * n_axes if n_axes else None
    return pltpu.CompilerParams(dimension_semantics=sem, vmem_limit_bytes=VMEM_LIMIT)


ANY = pl.BlockSpec(memory_space=pl.ANY)
SMEM = pl.BlockSpec(memory_space=pltpu.SMEM)


def all_of(a):
    return pl.BlockSpec(a.shape, lambda *_: (0,) * len(a.shape))


def corner(a):
    last = (min(a.shape[-2], 32 // a.dtype.itemsize), min(a.shape[-1], 128))
    return pl.BlockSpec((1,) * (a.ndim - 2) + last, lambda *_: (0,) * a.ndim)


def run(kernel, operands, specs, waits=(), prefetch=0, **kw):
    n, m = len(operands), len(waits)

    def body(*refs):
        return kernel(*refs[:n], *refs[n + m :])

    grid_spec = pltpu.PrefetchScalarGridSpec(
        num_scalar_prefetch=prefetch,
        grid=kw.pop("grid", (1,)),
        in_specs=[*specs, *[corner(a) for a in waits]],
        out_specs=kw.pop("out_specs"),
        scratch_shapes=kw.pop("scratch_shapes", ()),
    )
    return pl.pallas_call(body, grid_spec=grid_spec, **kw)(*operands, *waits)


class Blocks:
    def __init__(self, heads):
        self.heads = heads
        self.width = up128(heads * (HV + HQ))
        self.vals = heads * HV
        self.k0 = self.vals // 128 * 128
        self.kw = self.width - self.k0

    def stat(self, parts, i):
        return self.vals + i * 3 * (parts + 1)

    def window(self, i):
        wide = max(up128(j * HV % 128 + HV) for j in range(self.heads))
        first = i * HV
        return first, first // 128 * 128, wide


def lanes(shape, start=0):
    return lax.broadcasted_iota(jnp.int32, shape, len(shape) - 1) + start


def row(ref):
    return ref[...].reshape(1, -1)


def take(x, at, first):
    return jnp.sum(jnp.where((at >= first) & (at < first + 3), x, 0.0), axis=1, keepdims=True)


def three_terms(x):
    hi = x.astype(BF).astype(F32)
    mid = (x - hi).astype(BF).astype(F32)
    lo = (x - hi - mid).astype(BF).astype(F32)
    return hi, mid, lo


def norm_kernel(x_ref, g_ref, b_ref, r_ref, xh_ref, s_ref):
    step = min(256, x_ref.shape[1])

    @pl.loop(0, x_ref.shape[1] // step)
    def _(r):
        at = pl.ds(pl.multiple_of(r * step, step), step)
        x = x_ref[0, at, :].astype(F32)
        xc = x - jnp.mean(x, axis=1, keepdims=True)
        rstd = lax.rsqrt(jnp.mean(xc * xc, axis=1, keepdims=True) + EPS)
        xh = xc * rstd
        r_ref[0, at, :] = (xh * row(g_ref) + row(b_ref)).astype(BF)
        xh_ref[0, at, :] = xh.astype(BF)
        s_ref[0, at, :] = jnp.broadcast_to(rstd, (step, s_ref.shape[2]))


def byte_norm(x, g, b):
    seqs, slots, width = x.shape
    tile = min(1024, slots)
    at = lambda s, l: (s, l, 0)
    full = pl.BlockSpec((width,), lambda s, l: (0,))
    return pl.pallas_call(
        norm_kernel,
        grid=(seqs, slots // tile),
        in_specs=[pl.BlockSpec((1, tile, width), at), full, full],
        out_specs=[
            pl.BlockSpec((1, tile, width), at),
            pl.BlockSpec((1, tile, width), at),
            pl.BlockSpec((1, tile, 128), at),
        ],
        out_shape=[
            jax.ShapeDtypeStruct(x.shape, BF),
            jax.ShapeDtypeStruct(x.shape, BF),
            jax.ShapeDtypeStruct((seqs, slots, 128), F32),
        ],
        compiler_params=params(2),
        cost_estimate=cost(10 * x.size, 6 * x.size),
        name="byte_norm",
    )(x, g, b)


def pack_kernel(off, value_ref, key_ref, lat_ref, query_ref, out_ref, wide, tall, long):
    rows, vals = value_ref.shape
    tiles = wide.shape[1] // 128
    wide[...] = jnp.zeros_like(wide)
    wide[:, :vals] = value_ref[...].astype(F32)
    tall[...] = jnp.zeros_like(tall)
    tall[off : off + key_ref.shape[0]] = key_ref[...].astype(F32)
    long[...] = jnp.zeros_like(long)
    long[: lat_ref.shape[0]] = lat_ref[...].astype(F32)
    long[off : off + query_ref.shape[0]] = query_ref[...].astype(F32)
    for t in range(tiles):
        x = wide[:, t * 128 : (t + 1) * 128]
        if t == tiles - 1:
            x = x + tall[...].T
        out_ref[t * rows : (t + 1) * rows] = x.astype(BF)
    out_ref[tiles * rows :] = long[...].T.astype(BF)


def pack(blk, value, key, lat, query):
    rows, dl = value.shape[0], lat.shape[1]
    vm = pl.BlockSpec(memory_space=pltpu.VMEM)
    tiles = blk.width // 128
    return pl.pallas_call(
        partial(pack_kernel, blk.vals - blk.k0),
        in_specs=[vm] * 4,
        out_specs=vm,
        out_shape=jax.ShapeDtypeStruct((tiles * rows + dl, 128), BF),
        scratch_shapes=[
            pltpu.VMEM((rows, blk.width), F32),
            pltpu.VMEM((128, rows), F32),
            pltpu.VMEM((128, dl), F32),
        ],
        compiler_params=params(0),
        cost_estimate=cost(value.size, 8 * value.size),
        name="pack",
    )(value, key.T, lat, query.T)


def own_latent_kernel(dp_ref, near_ref, far_ref, out_ref, cols):
    dp = dp_ref[0]
    halves = near_ref.shape[0]
    nl, d = out_ref.shape
    dl = d // (2 * halves)
    base = near_ref.shape[1] - dl
    for slot in range(2 * halves):
        src = (far_ref if slot % 2 else near_ref).at[slot // 2]
        cols[pl.ds(pl.multiple_of((dp ^ slot) * dl, 16), dl), :] = src[base:].astype(F32)
    out_ref[...] = cols[...].T[:nl].astype(BF)


def own_latents(nl, d, dp, near, far):
    vm = pl.BlockSpec(memory_space=pltpu.VMEM)
    return pl.pallas_call(
        own_latent_kernel,
        in_specs=[pl.BlockSpec(memory_space=pltpu.SMEM), vm, vm],
        out_specs=vm,
        out_shape=jax.ShapeDtypeStruct((nl, d), BF),
        scratch_shapes=[pltpu.VMEM((d, 128), F32)],
        compiler_params=params(0),
        cost_estimate=cost(nl * d, 8 * nl * d),
        name="own_latents",
    )(dp, near, far)


def latent_kernel(parts, *refs):
    ins, (g_ref, b_ref, out_ref) = refs[:parts], refs[parts:]
    nl = ins[0].shape[0]
    for k in range(parts):
        x = ins[k][...].astype(F32)
        xc = x - jnp.mean(x, axis=1, keepdims=True)
        xh = xc * lax.rsqrt(jnp.mean(xc * xc, axis=1, keepdims=True) + EPS)
        out_ref[k * nl : (k + 1) * nl] = (xh * row(g_ref) + row(b_ref)).astype(BF)


def latent_norm(lats, g, b):
    nl, d = lats[0].shape
    vm = pl.BlockSpec(memory_space=pltpu.VMEM)
    return pl.pallas_call(
        partial(latent_kernel, len(lats)),
        in_specs=[vm] * (len(lats) + 2),
        out_specs=vm,
        out_shape=jax.ShapeDtypeStruct((nl * len(lats), d), BF),
        compiler_params=params(0),
        cost_estimate=cost(10 * nl * len(lats) * d, 4 * nl * len(lats) * d),
        name="latent_norm",
    )(*lats, g, b)


def fwd_kernel(
    blk, parts, tiles, sc_ref, b_ref, near_ref, far_ref, lat_ref, kv_ref, p_ref, y_ref, w_ref, q_ref, wq, acc, cs, st
):
    s = pl.program_id(0)
    n = acc.shape[0]
    nl = n // parts
    slots, width = b_ref.shape[1:]
    d = lat_ref.shape[1]
    me = sc_ref[pl.num_programs(0)]

    @pl.when(s == 0)
    def _():
        dp = sc_ref[pl.num_programs(0) + 1]
        halves = near_ref.shape[0]
        cw, dl = width // (2 * halves), d // (2 * halves)
        for slot in range(2 * halves):
            src = (far_ref if slot % 2 else near_ref).at[slot // 2]
            at = dp ^ slot
            for t in range(tiles):
                w_ref[pl.ds(pl.multiple_of(at * cw, 16), cw), t * 128 : (t + 1) * 128] = src[
                    t * cw : (t + 1) * cw
                ]
            wq[pl.ds(pl.multiple_of(at * dl, 16), dl), :] = src[tiles * cw : tiles * cw + dl]
        q = nn(lat_ref[...], wq[...]).astype(BF).astype(F32)
        at = lanes(q.shape, blk.k0)
        for i in range(blk.heads):
            key = blk.vals + i * HQ
            q_ref[i * n : (i + 1) * n] = jnp.where((at >= key) & (at < key + HQ), q, 0.0).astype(BF)

    kv_ref[0] = nn(b_ref[0], w_ref[...]).astype(BF)

    mask = lanes((n, slots)) < sc_ref[s]
    acc[...] = jnp.zeros_like(acc)
    st[...] = jnp.zeros_like(st)

    for i in range(blk.heads):
        first, start, wide = blk.window(i)
        rows = pl.ds(i * n, n)
        sc = nt(q_ref[rows, :], kv_ref[0, :, blk.k0 :])
        sc = jnp.where(mask, sc, NEGATIVE)
        top = jnp.max(sc, axis=1, keepdims=True)
        p = jnp.exp2((sc - top) * SCALE2)
        total = jnp.sum(p, axis=1, keepdims=True)
        p = (p * (1.0 / total)).astype(BF)
        p_ref[0, rows, :] = p
        o = nn(p, kv_ref[0, :, pl.ds(start, wide)])
        at = lanes((n, wide)) + start
        acc[:, pl.ds(start, wide)] += jnp.where((at >= first) & (at < first + HV), o, 0.0)
        lse = top * SCALE2 + jnp.log(total) * LOG2E
        at = lanes(st.shape, blk.k0)
        for j, term in enumerate(three_terms(lse)):
            st[...] = jnp.where(at == blk.vals + 3 * i + j, term, st[...])

    y = acc[...]
    center = jnp.mean(y, axis=0, keepdims=True).astype(BF).astype(F32)
    y = y - center
    low = (y[:, blk.k0 :] + st[...]).astype(BF)
    y = y.astype(BF)
    for k in range(parts):
        to = pl.ds(pl.multiple_of(s * nl, nl), nl)
        if blk.k0:
            y_ref[me ^ k, to, : blk.k0] = y[k * nl : (k + 1) * nl, : blk.k0]
        y_ref[me ^ k, to, blk.k0 :] = low[k * nl : (k + 1) * nl]
    cs[...] = jnp.where(lax.broadcasted_iota(jnp.int32, cs.shape, 0) == s, center, cs[...])

    @pl.when(s == pl.num_programs(0) - 1)
    def _():
        rows = lax.broadcasted_iota(jnp.int32, cs.shape, 0)
        c = jnp.where(rows < pl.num_programs(0), cs[...], 0.0).astype(BF)
        for k in range(parts):
            y_ref[k, y_ref.shape[1] - 16 :, :] = c


def attend(blk, parts, scalars, bytes_r, near, far, lat_r, waits):
    seqs, slots, width = bytes_r.shape
    n, d = lat_r.shape
    tiles = blk.width // 128
    rows = seqs * (n // parts) + 16
    seq = lambda s, sc: (s, 0, 0)
    flat = lambda s, sc: (0, 0)
    whole = lambda s, sc: (0, 0, 0)
    flops = 2 * seqs * slots * (width * blk.width + blk.heads * n * (blk.kw + 256))
    return run(
        partial(fwd_kernel, blk, parts, tiles),
        (scalars, bytes_r, near, far, lat_r),
        [
            pl.BlockSpec((1, slots, width), seq),
            pl.BlockSpec(near.shape, whole),
            pl.BlockSpec(far.shape, whole),
            pl.BlockSpec(lat_r.shape, flat),
        ],
        waits,
        prefetch=1,
        grid=(seqs,),
        out_specs=[
            pl.BlockSpec((1, slots, blk.width), seq),
            pl.BlockSpec((1, blk.heads * n, slots), seq),
            pl.BlockSpec((parts, rows, blk.width), whole),
            pl.BlockSpec((width, blk.width), flat),
            pl.BlockSpec((blk.heads * n, blk.kw), flat),
            pl.BlockSpec((d, 128), flat),
        ],
        scratch_shapes=[
            pltpu.VMEM((n, blk.width), F32),
            pltpu.VMEM((16, blk.width), F32),
            pltpu.VMEM((n, blk.kw), F32),
        ],
        out_shape=[
            jax.ShapeDtypeStruct((seqs, slots, blk.width), BF),
            jax.ShapeDtypeStruct((seqs, blk.heads * n, slots), BF),
            jax.ShapeDtypeStruct((parts, rows, blk.width), BF),
            jax.ShapeDtypeStruct((width, blk.width), BF),
            jax.ShapeDtypeStruct((blk.heads * n, blk.kw), BF),
            jax.ShapeDtypeStruct((d, 128), BF),
        ],
        compiler_params=params(1),
        cost_estimate=cost(flops, 4 * seqs * slots * width, seqs * blk.heads * n * slots),
        name="attend_forward",
    )


def rows_kernel(blk, parts, seqs, order, *refs):
    me_ref, *refs = refs
    pays, refs = refs[:parts], refs[parts:]
    lat_ref, cot_ref, g_ref, b_ref, bh_ref, bb_ref, w_hbm = refs[:7]
    outs, refs = refs[7 : 7 + len(order)], refs[7 + len(order) :]
    out_ref, lx_ref, rx_ref, lm_ref, rm_ref, vec_ref, dsum_ref = refs[:7]
    w_ref, mix, st, mid_s, acc, pay_ref, dbh, sums, total_s, sems = refs[7:]
    me = me_ref[0]
    rows, d = acc.shape
    nl = rows // seqs
    ff = w_hbm.shape[2]
    fw = blk.vals
    back0 = fw // 128 * 128
    shift = fw - back0
    back = slice(back0, back0 + blk.width)
    out0 = up128(2 * fw)
    wide = slice(0, blk.width)
    low = slice(out0, out0 + blk.width)

    def copies():
        for t in range(parts):
            yield pltpu.make_async_copy(w_hbm.at[t], w_ref.at[t], sems.at[0])

    for c in copies():
        c.start()
    @pl.loop(0, seqs)
    def _(s):
        sl = pl.ds(pl.multiple_of(s * nl, nl), nl)
        for j in range(parts):
            ys = [pays[k ^ j][me ^ k, sl, :].astype(F32) for k in range(parts)]
            at = lanes((nl, blk.kw), blk.k0)
            stat = jnp.zeros((nl, blk.kw), F32)
            weights = []
            for i in range(blk.heads):
                lse = [take(y[:, blk.k0 :], at, blk.vals + 3 * i) for y in ys]
                top = lse[0]
                for x in lse[1:]:
                    top = jnp.maximum(top, x)
                es = [jnp.exp2(x - top) for x in lse]
                total = sum(es[1:], es[0])
                weights.append([e / total for e in es])
                for k in range(parts):
                    for q, term in enumerate(three_terms(weights[i][k])):
                        stat = jnp.where(at == blk.stat(parts, i) + 3 * k + q, term, stat)
            st[j, sl, :] = stat
            at = lanes((nl, blk.width))
            pick = (lax.broadcasted_iota(jnp.int32, (nl, 16), 1) == s).astype(BF)
            m = jnp.zeros((nl, blk.width), F32)
            for k in range(parts):
                wt = jnp.zeros((nl, blk.width), F32)
                for i in range(blk.heads):
                    wt = jnp.where((at >= i * HV) & (at < (i + 1) * HV), weights[i][k], wt)
                m = m + (ys[k] + nn(pick, pays[k ^ j][me ^ k, seqs * nl :, :])) * wt
            m = jnp.where(at < blk.vals, m, 0.0)
            mix[j, sl, :] = m
            rm_ref[j, sl, :] = m.astype(BF)

    for c in copies():
        c.wait()

    acc[...] = jnp.zeros_like(acc)

    @pl.loop(0, parts)
    def _(j):
        acc[...] += nt(rm_ref[j], w_ref[me ^ j, :, low])

    def centred(x):
        xc = x - jnp.mean(x, axis=1, keepdims=True)
        rstd = lax.rsqrt(jnp.mean(xc * xc, axis=1, keepdims=True) + EPS)
        return xc * rstd, rstd

    @pl.loop(0, seqs)
    def _(s):
        sl = pl.ds(pl.multiple_of(s * nl, nl), nl)
        mid = acc[sl, :] + lat_ref[...].astype(F32)
        mid_s[sl, :] = mid
        lx_ref[0, sl, :] = (centred(mid)[0] * row(g_ref) + row(b_ref)).astype(BF)
        lx_ref[1, sl, :] = cot_ref[sl, :].astype(BF)
        out_ref[sl, :] = mid + row(bb_ref)
        acc[sl, :] = jnp.zeros((nl, d), F32)

    @pl.loop(0, parts)
    def _(j):
        t = me ^ j
        live = lanes((rows, blk.width)) < fw
        pre = nn(lx_ref[0], w_ref[t, :, wide]) + bh_ref[t]
        phi = 0.5 * (1.0 + lax.erf(pre * math.sqrt(0.5)))
        slope = phi + pre * (jnp.exp(-0.5 * pre * pre) * (1.0 / math.sqrt(2.0 * math.pi)))
        act = jnp.where(live, pre * phi, 0.0)
        rx_ref[1, j] = (pltpu.roll(act, shift, 1) if shift else act).astype(BF)
        dact = nn(lx_ref[1], w_ref[t, :, back])
        dact = pltpu.roll(dact, blk.width - shift, 1) if shift else dact
        dpre = jnp.where(live, dact * slope, 0.0).astype(BF)
        rx_ref[0, j] = dpre
        dbh[t] = jnp.sum(dpre.astype(F32), axis=0, keepdims=True)
        out_ref[...] += nt(rx_ref[1, j], w_ref[t, :, back])
        acc[...] += nt(rx_ref[0, j], w_ref[t, :, wide])

    off = blk.vals - blk.k0
    sums[...] = jnp.zeros_like(sums)
    total_s[...] = jnp.zeros_like(total_s)

    @pl.loop(0, seqs)
    def _(s):
        sl = pl.ds(pl.multiple_of(s * nl, nl), nl)
        xh, rstd = centred(mid_s[sl, :])
        dy, cot = acc[sl, :], cot_ref[sl, :]
        for i, v in enumerate((dy * xh, dy, cot)):
            sums[i : i + 1] += jnp.sum(v, axis=0, keepdims=True)
        e = dy * row(g_ref)
        dv = rstd * (
            e - jnp.mean(e, axis=1, keepdims=True) - xh * jnp.mean(e * xh, axis=1, keepdims=True)
        )
        dmid = cot + dv
        lm_ref[sl, :] = dmid.astype(BF)
        total_s[off : off + nl] += dmid

    dsum_ref[...] = total_s[...].T.astype(BF)
    cuts = d // 128
    for i in range(3):
        for c in range(cuts):
            vec_ref[i * cuts + c : i * cuts + c + 1] = sums[i : i + 1, c * 128 : (c + 1) * 128]
    vec_ref[3 * cuts :] = jnp.zeros((vec_ref.shape[0] - 3 * cuts, 128), F32)
    for t in range(parts):
        first, move = t * fw // 128, t * fw % 128
        v = jnp.concatenate([dbh[t], jnp.zeros((1, 128), F32)], axis=1)
        v = pltpu.roll(v, move, 1) if move else v
        for c in range(v.shape[1] // 128):
            if first + c < cuts:
                vec_ref[3 * cuts + first + c : 3 * cuts + first + c + 1] += v[:, c * 128 : (c + 1) * 128]

    @pl.loop(0, parts)
    def _(j):
        dm = nn(lm_ref[...], w_ref[me ^ j, :, low]).astype(BF)
        prod = dm.astype(F32) * mix[j]
        at = lanes(prod.shape)
        stat = st[j]
        at_k = lanes(stat.shape, blk.k0)
        for i in range(blk.heads):
            inner = jnp.sum(
                jnp.where((at >= i * HV) & (at < (i + 1) * HV), prod, 0.0), axis=1, keepdims=True
            )
            for q, term in enumerate(three_terms(inner)):
                stat = jnp.where(at_k == blk.stat(parts, i) + 3 * parts + q, term, stat)
        if blk.k0:
            pay_ref[j, :, : blk.k0] = dm[:, : blk.k0]
        pay_ref[j, :, blk.k0 :] = jnp.where(at_k < blk.vals, dm[:, blk.k0 :].astype(F32), stat).astype(BF)

    for out, stages in zip(outs, order, strict=True):
        for i, stage in enumerate(stages):
            for k in range(parts):
                out[me ^ k, i] = pay_ref[stage ^ k]


def rows_step(blk, parts, seqs, order, me, pays, lat, cot, g, b, bh, bb, w):
    rows, d = cot.shape
    nl = rows // seqs
    whole = lambda a: pl.BlockSpec(a.shape, lambda i, me, r=len(a.shape): (0,) * r)
    outs = [jax.ShapeDtypeStruct((parts, len(o), rows, blk.width), BF) for o in order] + [
        jax.ShapeDtypeStruct((rows, d), F32),
        jax.ShapeDtypeStruct((2, rows, d), BF),
        jax.ShapeDtypeStruct((2, parts, rows, blk.width), BF),
        jax.ShapeDtypeStruct((rows, d), BF),
        jax.ShapeDtypeStruct((parts, rows, blk.width), BF),
        jax.ShapeDtypeStruct(((4 * d // 128 + 7) // 8 * 8, 128), F32),
        jax.ShapeDtypeStruct((d, 128), BF),
    ]
    return pl.pallas_call(
        partial(rows_kernel, blk, parts, seqs, order),
        grid_spec=pltpu.PrefetchScalarGridSpec(
            num_scalar_prefetch=1,
            grid=(1,),
            in_specs=[whole(a) for a in pays]
            + [whole(a) for a in (lat, cot, g, b, bh, bb)]
            + [ANY],
            out_specs=[whole(o) for o in outs],
            scratch_shapes=[
                pltpu.VMEM((parts, d, w.shape[-1]), BF),
                pltpu.VMEM((parts, rows, blk.width), F32),
                pltpu.VMEM((parts, rows, blk.kw), F32),
                pltpu.VMEM((rows, d), F32),
                pltpu.VMEM((rows, d), F32),
                pltpu.VMEM((parts, rows, blk.width), BF),
                pltpu.VMEM((parts, 1, blk.width), F32),
                pltpu.VMEM((8, d), F32),
                pltpu.VMEM((128, d), F32),
                pltpu.SemaphoreType.DMA((1,)),
            ],
        ),
        out_shape=outs,
        compiler_params=params(1),
        cost_estimate=cost(12 * rows * d * d, 2 * w.size + 40 * rows * d, 2 * rows * d),
        name="rows",
    )(me, *pays, lat, cot, g, b, bh, bb, w)


def ff_kernel(blk, me_ref, lh_ref, lo_ref, rd_ref, ra_ref, out_ref):
    fw = blk.vals
    back0 = fw // 128 * 128
    hid = tn(lh_ref[0], rd_ref[0, 0])
    back = tn(lo_ref[0], ra_ref[0, 0])
    dps, _, dl, wide = out_ref.shape
    cuts = [(0, back0, hid[:, :back0])] if back0 else []
    if back0 < blk.width:
        n = blk.width - back0
        cuts.append((back0, n, hid[:, back0:] + back[:, :n]))
        cuts.append((blk.width, wide - blk.width, back[:, n : n + wide - blk.width]))
    for at, n, piece in cuts:
        if n:
            out_ref[:, 0, :, at : at + n] = piece.astype(BF).reshape(dps, dl, n)


def ff_grads(blk, me, dps, lx, rx):
    _, parts, rows, width = rx.shape
    d = lx.shape[2]
    wide = up128(2 * blk.vals)
    return pl.pallas_call(
        partial(ff_kernel, blk),
        grid_spec=pltpu.PrefetchScalarGridSpec(
            num_scalar_prefetch=1,
            grid=(parts,),
            in_specs=[
                pl.BlockSpec((1, rows, d), lambda i, me: (0, 0, 0)),
                pl.BlockSpec((1, rows, d), lambda i, me: (1, 0, 0)),
                pl.BlockSpec((1, 1, rows, width), lambda i, me: (0, i, 0, 0)),
                pl.BlockSpec((1, 1, rows, width), lambda i, me: (1, i, 0, 0)),
            ],
            out_specs=pl.BlockSpec((dps, 1, d // dps, wide), lambda i, me: (0, me[0] ^ i, 0, 0)),
        ),
        out_shape=jax.ShapeDtypeStruct((dps, parts, d // dps, wide), BF),
        compiler_params=params(1),
        cost_estimate=cost(4 * parts * rows * d * width, 4 * parts * d * width),
        name="ff_grads",
    )(me, lx, lx, rx, rx)


def slot_place(slot, dps):
    return (slot & 1) * (dps // 2) + (slot >> 1)


def core_slot(core, i, half):
    return core * half + ((i ^ (1 - core)) if half > 1 else i)


def out_kernel(half, dps, sc_ref, lx_ref, rx_ref, lx2_ref, rx2_ref, *outs):
    core, dp = sc_ref[0], sc_ref[1]
    dl = lx_ref.shape[1] // dps
    for i, out_ref in enumerate(outs):
        slot = core_slot(core, i, half)
        r = (tn(lx_ref[...], rx_ref[slot]) + tn(lx2_ref[...], rx2_ref[slot])).astype(BF)
        for z in range(dps):
            out_ref[slot_place(dp ^ z, dps)] = r[z * dl : (z + 1) * dl]


def out_grads(scalars, dps, lx, rx, lx2, rx2, waits):
    parts, rows, width = rx.shape
    d = lx.shape[1]
    half = max(parts // 2, 1)
    whole = lambda a: pl.BlockSpec(a.shape, lambda i, sc, r=len(a.shape): (0,) * r)
    outs = [jax.ShapeDtypeStruct((dps, d // dps, width), BF)] * half
    return run(
        partial(out_kernel, half, dps),
        (scalars, lx, rx, lx2, rx2),
        [whole(a) for a in (lx, rx, lx2, rx2)],
        waits,
        prefetch=1,
        out_specs=[whole(o) for o in outs],
        out_shape=outs,
        compiler_params=params(1),
        cost_estimate=cost(4 * half * rows * d * width, 2 * half * d * width),
        name="out_grads",
    )


def bwd_kernel(blk, parts, dps, ks, add, before, sc_ref, *refs):
    count = len(ks)
    kvs, ps, qs, ws, refs = (
        refs[:count],
        refs[count : 2 * count],
        refs[2 * count : 3 * count],
        refs[3 * count : 4 * count],
        refs[4 * count :],
    )
    xh_ref, g_ref, b_ref, dm_ref, *refs = refs
    extra, refs = refs[:add], refs[add:]
    earlier, refs = (refs[: 2 * before + 1], refs[2 * before + 1 :]) if add else ((), refs)
    dkvs, gws, refs = refs[:count], refs[count : 2 * count], refs[2 * count :]
    *sums, dkvt, gacc, sacc, dmx, dqs, dqg = refs
    me, dp = sc_ref[0], sc_ref[1]
    s = pl.program_id(0)
    n = dmx.shape[1]
    nl = n // parts
    off, qk = blk.vals - blk.k0, blk.heads * HQ

    @pl.when(s == 0)
    def _():
        gacc[...] = jnp.zeros_like(gacc)
        sacc[...] = jnp.zeros_like(sacc)
        dqs[...] = jnp.zeros_like(dqs)

    for c in range(count):
        kv_ref, p_ref = kvs[c], ps[c]
        for k in range(parts):
            dmx[c, k * nl : (k + 1) * nl] = dm_ref[me ^ k, c]
        tail = dmx[c, :, blk.k0 :].astype(F32)
        at_k = lanes(tail.shape, blk.k0)
        at_n = lax.broadcasted_iota(jnp.int32, (n, 1), 0)
        dkvt[c] = jnp.zeros_like(dkvt[c])
        for i in range(blk.heads):
            first, start, width = blk.window(i)
            rows = pl.ds(i * n, n)
            cols = pl.ds(start, width)
            stat = blk.stat(parts, i)
            ratio = take(tail, at_k, stat)
            for k in range(1, parts):
                ratio = jnp.where(at_n >= k * nl, take(tail, at_k, stat + 3 * k), ratio)
            inner = take(tail, at_k, stat + 3 * parts)
            at = lanes((n, width)) + start
            dm = dmx[c, :, cols].astype(F32)
            dm = jnp.where((at >= first) & (at < first + HV), dm, 0.0)
            dpr = nt(dm.astype(BF), kv_ref[0, :, cols])
            ds = (p_ref[0, rows, :].astype(F32) * ((dpr - inner) * (ratio * SCALE))).astype(BF)
            dkvt[c, cols, :] += tn((dm * ratio).astype(BF), p_ref[0, rows, :])
            dkvt[c, blk.k0 :, :] += tn(qs[c][rows, :], ds)
            dq = nn(ds, kv_ref[0, :, blk.k0 :])
            key = blk.vals + i * HQ
            dqs[c] += jnp.where((at_k >= key) & (at_k < key + HQ), dq, 0.0)

        low = dkvt[c].astype(BF)
        dkvs[c][0] = low.T
        gacc[c] += nn(low, xh_ref[0])
        sacc[c] += jnp.sum(low.astype(F32), axis=1, keepdims=True)

    @pl.when(s == pl.num_programs(0) - 1)
    def _():
        dg, db = 0.0, 0.0
        for c in range(count):
            wt = ws[c][...].T.astype(F32)
            grad, col = gacc[c], sacc[c, :, 0:1]
            dg = dg + jnp.sum(wt * grad, axis=0, keepdims=True)
            db = db + jnp.sum(wt * col, axis=0, keepdims=True)
            gw = (grad * row(g_ref) + col * row(b_ref)).T.astype(BF)
            cl = gw.shape[0] // dps
            for z in range(dps):
                gws[c][slot_place(dp ^ z, dps), :cl] = gw[z * cl : (z + 1) * cl]
            if add and c == count - 1:
                more = jnp.where(dp % 2 == 0, extra[0][...].astype(F32), 0.0)
                for e in extra[1:-1]:
                    more = more + e[...].astype(F32)
                gws[c][:, cl:] = more.astype(BF)
                dl = extra[-1].shape[0] // dps
                for z in range(dps):
                    to = slot_place(dp ^ z, dps)
                    beside = gws[c][to, cl:, blk.k0 :].astype(F32) + extra[-1][z * dl : (z + 1) * dl].astype(F32)
                    gws[c][to, cl:, blk.k0 :] = beside.astype(BF)
            for k in range(parts):
                dqg[pl.ds(pl.multiple_of((me ^ k) * nl, 8), nl), :] = dqs[c, k * nl : (k + 1) * nl]
            left = pltpu.roll(dqg[: n // 2], (128 - off) % 128, 1)
            right = pltpu.roll(dqg[n // 2 :], (64 - off) % 128, 1)
            dqs[c, : n // 2] = left + right
        head = parts * (n // 2)
        if add:
            (msg,) = sums
            gains = earlier[2 * before].shape[0]
            first = msg.shape[0] - gains
            msg[:head] = sum((r[...] for r in earlier[1:before]), earlier[0][...]) if before else jnp.zeros((head, 128), F32)
            msg[head:first] = (
                sum((r[...] for r in earlier[before + 1 : 2 * before]), earlier[before][...])
                if before
                else jnp.zeros((first - head, 128), F32)
            )
            msg[first:] = earlier[2 * before][...]
            at, gain = msg, head
        else:
            at, small = sums
            at[...] = jnp.zeros_like(at)
            small[...] = jnp.zeros_like(small)
        for c, k in enumerate(ks):
            at[pl.ds(pl.multiple_of((me ^ k) * (n // 2), 8), n // 2), :] += dqs[c, : n // 2]
        if add:
            small, base = msg, gain
        else:
            base = 0
        cuts = dg.shape[1] // 128
        for i, v in enumerate((dg, db)):
            for c in range(cuts):
                r = base + i * cuts + c
                small[r : r + 1] += v[:, c * 128 : (c + 1) * 128]


def attend_backward(blk, parts, dps, ks, scalars, kvs, ps, qs, ws, xh, g, b, pay, extra, earlier, waits):
    seqs, slots, width = xh.shape
    count = len(kvs)
    n = qs[0].shape[0] // blk.heads
    nl = n // parts
    seq = lambda s, sc: (s, 0, 0)
    cl = width // dps
    sizes = [cl] * count
    if extra:
        sizes[-1] += extra[0].shape[1]
    outs = (
        [jax.ShapeDtypeStruct((seqs, slots, blk.width), BF)] * count
        + [jax.ShapeDtypeStruct((dps, r, blk.width), BF) for r in sizes]
    )
    head, gains = parts * (n // 2), (2 * width // 128 + 7) // 8 * 8
    if extra:
        outs = outs + [jax.ShapeDtypeStruct((head + gains + earlier[-1].shape[0], 128), F32)]
    else:
        outs = outs + [jax.ShapeDtypeStruct((head, 128), F32), jax.ShapeDtypeStruct((gains, 128), F32)]
    res = run(
        partial(bwd_kernel, blk, parts, dps, tuple(ks), len(extra), len(earlier) // 2),
        (scalars, *kvs, *ps, *qs, *ws, xh, g, b, pay, *extra, *earlier),
        [pl.BlockSpec((1, slots, blk.width), seq)] * count
        + [pl.BlockSpec((1, blk.heads * n, slots), seq)] * count
        + [all_of(a) for a in (*qs, *ws)]
        + [
            pl.BlockSpec((1, slots, width), seq),
            all_of(g),
            all_of(b),
            pl.BlockSpec((parts, count, nl, blk.width), lambda s, sc: (0, 0, s, 0)),
        ]
        + [all_of(a) for a in (*extra, *earlier)],
        waits,
        prefetch=1,
        grid=(seqs,),
        out_specs=[pl.BlockSpec((1, slots, blk.width), seq)] * count + [all_of(o) for o in outs[count:]],
        scratch_shapes=[
            pltpu.VMEM((count, blk.width, slots), F32),
            pltpu.VMEM((count, blk.width, width), F32),
            pltpu.VMEM((count, blk.width, 128), F32),
            pltpu.VMEM((count, n, blk.width), BF),
            pltpu.VMEM((count, n, blk.kw), F32),
            pltpu.VMEM((n, blk.kw), F32),
        ],
        out_shape=outs,
        compiler_params=params(1),
        cost_estimate=cost(
            2 * count * seqs * slots * (width * blk.width + 4 * blk.heads * n * 256),
            (2 + 4 * count) * seqs * slots * width,
        ),
        name="attend_backward",
    )
    return res[:count], res[count : 2 * count], res[2 * count :]


def bytes_kernel(parts, *refs):
    dkvs, ws = refs[:parts], refs[parts : 2 * parts]
    xh_ref, s_ref, g_ref, *_, out_ref, done_ref = refs[2 * parts :]
    done_ref[...] = jnp.zeros_like(done_ref)
    step = min(256, out_ref.shape[1])

    @pl.loop(0, out_ref.shape[1] // step)
    def _(r):
        at = pl.ds(pl.multiple_of(r * step, step), step)
        dy = nt(dkvs[0][0, at, :], ws[0][...])
        for k in range(1, parts):
            dy = dy + nt(dkvs[k][0, at, :], ws[k][...])
        xh = xh_ref[0, at, :].astype(F32)
        e = dy * row(g_ref)
        me = jnp.mean(e, axis=1, keepdims=True)
        mx = jnp.mean(e * xh, axis=1, keepdims=True)
        out_ref[0, at, :] = s_ref[0, at, 0:1] * (e - me - xh * mx)


def byte_grads(first, count, dkvs, ws, xh, rstd, g, into, waits):
    _, slots, width = xh.shape
    bw = ws[0].shape[1]
    tile = min(512, slots)
    at = lambda s, l: (first + s, l, 0)
    flat = lambda s, l: (0, 0)
    kept = [] if into is None else [into]
    return run(
        partial(bytes_kernel, len(ws)),
        (*dkvs, *ws, xh, rstd, g, *kept),
        [pl.BlockSpec((1, tile, bw), at) for _ in dkvs]
        + [pl.BlockSpec((width, bw), flat) for _ in ws]
        + [
            pl.BlockSpec((1, tile, width), at),
            pl.BlockSpec((1, tile, 128), at),
            all_of(g),
        ]
        + [ANY] * len(kept),
        waits,
        grid=(count, slots // tile),
        out_specs=[pl.BlockSpec((1, tile, width), at), pl.BlockSpec((8, 128), flat)],
        out_shape=[jax.ShapeDtypeStruct(xh.shape, F32), jax.ShapeDtypeStruct((8, 128), BF)],
        input_output_aliases={2 * len(ws) + 3: 0} if kept else {},
        compiler_params=params(2),
        cost_estimate=cost(2 * count * slots * width * bw * len(ws), 10 * count * slots * width),
        name="byte_grads",
    )


def merge_kernel(cl, own_ref, *refs):
    more, (keep_ref, send_ref) = refs[:-2], refs[-2:]
    h = keep_ref.shape[0]
    for i in range(2 * h):
        out, at = (keep_ref, i) if i < h else (send_ref, i - h)
        x = own_ref[i, :cl].astype(F32)
        for r in more:
            x = x + r[i].astype(F32)
        out[at, :cl] = x.astype(BF)
        out[at, cl:] = own_ref[i, cl:]


def merge(own, more, waits):
    dps, rows, bw = own.shape
    cl = more[0].shape[1]
    out = jax.ShapeDtypeStruct((dps // 2, rows, bw), BF)
    return run(
        partial(merge_kernel, cl),
        (own, *more),
        [all_of(a) for a in (own, *more)],
        waits,
        out_specs=[all_of(out)] * 2,
        out_shape=[out] * 2,
        compiler_params=params(1),
        cost_estimate=cost(own.size * len(more), own.size * 6),
        name="merge",
    )


def plus_kernel(a_ref, b_ref, out_ref):
    out_ref[...] = a_ref[...] + b_ref[...]


def plus(a, b, waits):
    return run(
        plus_kernel,
        (a, b),
        [all_of(a)] * 2,
        waits,
        out_specs=all_of(a),
        out_shape=jax.ShapeDtypeStruct(a.shape, a.dtype),
        compiler_params=params(1),
        cost_estimate=cost(a.size, 12 * a.size),
        name="plus",
    )


def split_kernel(keep_ref, got_ref, own_ref, *outs):
    own_ref[...] = keep_ref[0].astype(F32) + got_ref[0].astype(F32)
    for z, out in enumerate(outs):
        out[...] = (keep_ref[z + 1].astype(F32) + got_ref[z + 1].astype(F32)).astype(BF)


def split(keep, got):
    h, rows, bw = keep.shape
    vm = pl.BlockSpec(memory_space=pltpu.VMEM)
    return pl.pallas_call(
        split_kernel,
        in_specs=[vm, vm],
        out_specs=[vm] * h,
        out_shape=[jax.ShapeDtypeStruct((rows, bw), F32)] + [jax.ShapeDtypeStruct((rows, bw), BF)] * (h - 1),
        compiler_params=params(0),
        cost_estimate=cost(keep.size, keep.size * 6),
        name="split",
    )(keep, got)


def final_kernel(blk, parts, dps, near, sc_ref, *refs):
    own_ref, refs = refs[0], refs[1:]
    gots, refs = refs[:near], refs[near:]
    ff_ref, msg_ref, refs = refs[0], refs[1], refs[2:]
    lat_refs, lqs, refs = refs[:parts], refs[parts : 2 * parts], refs[2 * parts :]
    g_ref, b_ref, gv_ref, gk_ref, go_ref, gh_ref, gb_ref, gq_ref, gl_ref, sg_ref, sb_ref, *vecs = refs[:-3]
    dys, tr, dqx = refs[-3:]
    me, dp = sc_ref[0], sc_ref[1]
    nl, d = lat_refs[0].shape
    n = nl * parts
    h = n // 2
    dl = d // dps
    off, qk, fw = blk.vals - blk.k0, blk.heads * HQ, blk.vals
    total = own_ref[...]
    for r in gots:
        total = total + r[...].astype(F32)
    cl = gv_ref.shape[0]
    gv_ref[...] = total[:cl, : blk.vals]
    gk_ref[...] = total[:cl, blk.k0 :].T[off : off + qk]
    go_ref[...] = total[cl:, :fw]
    rows_sum = total[cl:, blk.k0 :].T[off : off + nl]
    both = ff_ref[0].astype(F32)
    for k in range(1, parts):
        both = both + ff_ref[k].astype(F32)
    gh_ref[...] = both[:, :fw]
    back0 = fw // 128 * 128
    tail = both[:, back0:]
    shift = fw - back0
    tail = pltpu.roll(tail, tail.shape[1] - shift, 1) if shift else tail
    gb_ref[...] = tail[:, :fw]
    at = lanes((h, 128))
    dys[...] = jnp.zeros_like(dys)
    for k in reversed(range(parts)):
        block = msg_ref[pl.ds(pl.multiple_of((me ^ k) * h, 8), h), :]
        dqx[:h] = pltpu.roll(jnp.where(at < 64, block, 0.0), off, 1)
        dqx[h:] = pltpu.roll(jnp.where(at >= 64, block, 0.0), (off + 64) % 128, 1)
        dys[...] += nt(dqx[...].astype(BF), lqs[k][...])
    g, b = row(g_ref), row(b_ref)
    dg, db = jnp.zeros((1, d), F32), jnp.zeros((1, d), F32)
    for k in range(parts):
        rows = pl.ds(pl.multiple_of((me ^ k) * nl, 8), nl)
        x = lat_refs[k][...].astype(F32)
        xc = x - jnp.mean(x, axis=1, keepdims=True)
        rs = lax.rsqrt(jnp.mean(xc * xc, axis=1, keepdims=True) + EPS)
        xh = xc * rs
        dy = dys[rows, :]
        dg = dg + jnp.sum(dy * xh, axis=0, keepdims=True)
        db = db + jnp.sum(dy, axis=0, keepdims=True)
        if k == 0:
            e = dy * g
            keep = rs * (
                e - jnp.mean(e, axis=1, keepdims=True) - xh * jnp.mean(e * xh, axis=1, keepdims=True)
            )
        dys[rows, :] = xh * g + b
    sg_ref[...] = dg[0]
    sb_ref[...] = db[0]
    tr[...] = dys[...].T
    here = pl.ds(pl.multiple_of(dp * dl, 8), dl)
    mine = tr[here, :].astype(BF)
    gq = lax.dot_general(dqx[...].astype(BF), mine, (((0,), (1,)), ((), ())), preferred_element_type=F32)
    gq_ref[...] = gq[off : off + qk]
    tr[:, :nl] = keep.T
    gl_ref[...] = tr[here, :nl].T + rows_sum
    first = parts * h
    gains = (2 * vecs[0].shape[0] // 128 + 7) // 8 * 8
    start = first
    for i, ref in enumerate(vecs):
        if i == 2:
            start = first + gains
        for c in range(ref.shape[0] // 128):
            ref[c * 128 : (c + 1) * 128] = msg_ref[start + c : start + c + 1].reshape(128)
        start += ref.shape[0] // 128


def final(blk, dps, scalars, own, gots, ff, msg, lats, lqs, g, b, width, cl):
    parts = len(lats)
    nl, d = lats[0].shape
    n = nl * parts
    dl = d // dps
    qk, fw = blk.heads * HQ, blk.vals
    vm = pl.BlockSpec(memory_space=pltpu.VMEM)
    shapes = [(cl, blk.vals), (qk, cl), (dl, fw), (dl, fw), (dl, fw), (qk, dl), (nl, dl), (d,), (d,)]
    shapes += [(width,), (width,), (d,), (d,), (d,), (d,)]
    return pl.pallas_call(
        partial(final_kernel, blk, parts, dps, len(gots)),
        in_specs=[SMEM] + [vm] * (5 + len(gots) + 2 * parts),
        out_specs=[vm] * len(shapes),
        out_shape=[jax.ShapeDtypeStruct(s, F32) for s in shapes],
        scratch_shapes=[pltpu.VMEM((n, d), F32), pltpu.VMEM((d, n), F32), pltpu.VMEM((n, 128), F32)],
        compiler_params=params(0),
        cost_estimate=cost(2 * n * 128 * d * parts, 12 * d * n),
        name="final",
    )(scalars, own, *gots, ff, msg, *lats, *lqs, g, b)


def on_device(
    dps,
    parts,
    byte_in,
    lengths,
    latent,
    g_in,
    b_in,
    g_lat,
    b_lat,
    w_query,
    w_key,
    w_value,
    w_out,
    g_mlp,
    b_mlp,
    w_hidden,
    b_hidden,
    w_back,
    b_back,
    cotangent,
):
    seqs, slots, width = byte_in.shape
    nl, dl = latent.shape
    n, d = nl * parts, dl * dps
    blk = Blocks(w_key.shape[1] // HQ)
    qk = w_key.shape[1]
    bw = blk.width
    me = lax.axis_index("tensor").astype(jnp.int32)
    dp = lax.axis_index("dp").astype(jnp.int32)
    core = dp % 2

    def hop(x, k):
        return lax.ppermute(x, "tensor", [(i, i ^ k) for i in range(parts)])

    def hop_dp(x, k):
        return lax.ppermute(x, "dp", [(i, i ^ k) for i in range(dps)])

    def swap(x):
        return lax.all_to_all(x, "tensor", split_axis=0, concat_axis=0, tiled=True)

    def widen(x):
        return jnp.pad(x, ((0, 0), (0, bw - x.shape[1])))

    def after(x, *others):
        return lax.optimization_barrier((x, *others))[0]

    fw = d // parts
    mats = jnp.concatenate([w_hidden, w_back.T], axis=1)
    mats = jnp.pad(mats, ((0, 0), (0, up128(2 * fw) - 2 * fw)))
    mats = jnp.concatenate([mats, widen(w_out.T)], axis=1)

    tiles = bw // 128
    off = blk.vals - blk.k0
    dp1, me1 = dp.reshape(1), me.reshape(1)
    shard = pack(blk, w_value, w_key, latent, w_query)
    got = [hop_dp(shard, j) for j in range(2, dps, 2)]
    bytes_r, xh, rstd = byte_norm(after(byte_in, shard), g_in, b_in)
    near = after(jnp.stack([shard] + got, axis=0), rstd)
    far = hop_dp(near, 1)
    lat = own_latents(nl, d, dp1, near, far)
    lats = [lat] + [hop(lat, k) for k in range(1, parts)]
    lat_r = latent_norm(lats, g_lat, b_lat)
    gate = lax.optimization_barrier((near, far, *lats))
    nears = [near] + [hop(gate[0], k) for k in range(1, parts)]
    fars = [far]
    mats = lax.all_gather(after(mats, gate[0]), ("tensor", "dp"), axis=0, tiled=True).reshape(parts, d, -1)

    live = jnp.clip(lengths - me * slots, 0, slots).astype(jnp.int32)
    scalars = jnp.concatenate([live, me1, dp1])
    kvs, ps, ws, qs, lqs, pays = [], [], [], [], [], []
    for k in range(parts):
        waits = []
        if k == 1:
            late = lax.optimization_barrier((kvs[0], *nears[1:]))[1:]
            fars += [hop_dp(a, 1) for a in late]
        if k:
            waits.append(kvs[k - 1])
        if k > 1:
            waits.append(pays[k - 2])
        kv, p, y, w, q, lq = attend(blk, parts, scalars, bytes_r, nears[k], fars[k], lat_r, waits)
        kvs.append(kv)
        ps.append(p)
        ws.append(w)
        qs.append(q)
        lqs.append(lq)
        pays.append(swap(y))

    rows = seqs * nl
    bh = jnp.pad(b_hidden.reshape(parts, 1, -1), ((0, 0), (0, 0), (0, bw - fw)))
    slots_left = list(range(1, parts)) + [0]
    order = [slots_left[i : i + 2] for i in range(0, parts, 2)]
    res = rows_step(
        blk,
        parts,
        seqs,
        order,
        jnp.stack([me, core]),
        pays,
        lat,
        cotangent.reshape(rows, d),
        g_mlp,
        b_mlp,
        bh,
        b_back,
        mats,
    )
    dpays, (out, lx, rx, lm, rm, vec_rows, dsum) = res[: len(order)], res[len(order) :]
    latents_out = out.reshape(seqs, nl, d)
    dpays = [swap(a) for a in dpays]
    lm2, rm2 = hop_dp(lm, 1), hop_dp(rm, 1)
    ff = ff_grads(blk, me1, dps, lx, rx)
    scalars = jnp.stack([me, dp])
    pairs = out_grads(jnp.stack([core, dp]), dps, lm, rm, lm2, rm2, [ff])
    half = len(pairs)
    moved = []
    for i in range(half):
        perm = []
        for z in range(dps):
            for t in range(parts):
                c = z % 2
                slot = c * half + ((i ^ (1 - c)) if half > 1 else i)
                if slot:
                    perm.append((z * parts + t, z * parts + (t ^ slot)))
        moved.append(lax.ppermute(pairs[i], ("dp", "tensor"), perm))
    ff = lax.psum_scatter(ff, "dp", scatter_dimension=0, tiled=True).reshape(parts, dl, -1)

    dkvs, gws, dqs, dgbs = [None] * parts, [None] * parts, [], []
    for at, ks in enumerate(order):
        last = at == len(order) - 1
        got, grads, sums = attend_backward(
            blk,
            parts,
            dps,
            ks,
            scalars,
            [kvs[k] for k in ks],
            [ps[k] for k in ks],
            [qs[k] for k in ks],
            [ws[k] for k in ks],
            xh,
            g_in,
            b_in,
            dpays[at],
            [pairs[min(1, half - 1)], *moved, dsum] if last else [],
            [*dqs, *dgbs, vec_rows] if last else [],
            [pairs[0]] if at == 0 else [],
        )
        for i, k in enumerate(ks):
            dkvs[k] = got[i]
            gws[k] = hop(grads[i], k) if k else grads[i]
        if not last:
            dqs.append(sums[0])
            dgbs.append(sums[1])
    (msg,) = sums

    cl = width // dps
    h = dps // 2
    wide_steps = [(hop_dp, 2**i) for i in reversed(range(1, dps.bit_length() - 1))]
    steps = [(hop_dp, 1), wide_steps[0]] + [(hop, 2**i) for i in range(parts.bit_length() - 1)] + wide_steps[1:]
    grad_bytes = None
    group = max(seqs // 2, 1)
    todo = list(range(0, seqs, group))
    done = []

    def cover(*waits):
        nonlocal grad_bytes, done
        if todo:
            grad_bytes, token = byte_grads(todo.pop(0), group, dkvs, ws, xh, rstd, g_in, grad_bytes, waits)
            done = [token]

    def sent(msg):
        f, j = steps.pop(0)
        return f(msg, j)

    msg = msg + sent(msg)
    got = sent(msg)
    cover(msg, *[gws[k] for ks in order[:-1] for k in ks])
    keep, send = merge(gws[0], [gws[k] for ks in order for k in ks if k], [*done, got])
    far = hop_dp(send, 1)
    msg = plus(msg, got, done)
    other = sent(msg)
    own, *low = split(keep, far)
    got = [hop_dp(low[z - 1], 2 * z) for z in range(1, h)]
    ff = swap(ff)
    while todo:
        cover(msg, *low)
    msg = plus(msg, other, [*done, *got])
    while steps:
        msg = msg + sent(msg)

    gv, gk, go, gh, gb, gq, gl, sum_g_lat, sum_b_lat, sum_g_in, sum_b_in, sum_g_mlp, sum_b_mlp, sum_back, sum_hidden = final(
        blk, dps, scalars, own, got, ff, msg, lats, lqs, g_lat, b_lat, width, cl
    )
    return (
        latents_out,
        grad_bytes,
        gl,
        sum_g_in,
        sum_b_in,
        sum_g_lat,
        sum_b_lat,
        gq.T,
        gk.T,
        gv,
        go.T,
        sum_g_mlp,
        sum_b_mlp,
        gh,
        sum_hidden,
        gb.T,
        sum_back,
    )


def solution(mesh):
    return jax.shard_map(
        partial(on_device, mesh.shape["dp"], mesh.shape["tensor"]),
        mesh=mesh,
        in_specs=(
            P("dp", "tensor", None),
            P("dp"),
            P("tensor", "dp"),
            P(),
            P(),
            P(),
            P(),
            P("dp", "tensor"),
            P("dp", "tensor"),
            P("dp", "tensor"),
            P("tensor", "dp"),
            P(),
            P(),
            P("dp", "tensor"),
            P(),
            P("tensor", "dp"),
            P(),
            P("dp", "tensor", None),
        ),
        out_specs=(
            P("dp", "tensor", None),
            P("dp", "tensor", None),
            P("tensor", "dp"),
            P(),
            P(),
            P(),
            P(),
            P("dp", "tensor"),
            P("dp", "tensor"),
            P("dp", "tensor"),
            P("tensor", "dp"),
            P(),
            P(),
            P("dp", "tensor"),
            P(),
            P("tensor", "dp"),
            P(),
        ),
        check_vma=False,
    )
```
